32 devices in a mesh: energy: 8 (over z, core), layer: 4 (over y, x).
Axes of the slice: x: 2, y: 2, z: 4, core: 2. Of those that a mesh axis runs over, the one named last changes fastest.
Arguments:
- green_blocks: bfloat16 [8, 12, 12, 1536], P('energy', None, None, 'layer'), as said below
- coupling: bfloat16 [12, 12, 4, 1536], P(None, None, None, 'layer'), may hold values from -1.75 to 1.75
- phonon_weights: float32 [2, 48, 4, 1536], P(None, None, None, 'layer'), may hold values from 0.001 to 0.01
- neighbours: int32 [4, 1536], P(None, 'layer'), may hold values from 0 to 1151, as said below
- phonon_shifts: int32 [48], replicated, may hold values from 1 to 2
Outputs:
- corrected: bfloat16 [8, 12, 12, 1536], P('energy', None, None, 'layer')
- polarization: float32 [48, 4, 1536], P(None, None, ('layer', 'energy'))
The draws below stay inside these ranges and needn't reach their ends.
Inputs may be any that keep to these rules, and one draw needn't show every extreme that they name: Every 12 x 12 block green_blocks[E, :, :, a] is symmetric. neighbours[k, a] is a place in the window of atom a: places 0 to 383 are the previous layer block, then the own block, then the next one. Slot 0 lies in the previous block, slot 1 in the next block, the other slots in the own block and never name the atom itself.
All inputs are finite; a program needn't handle non-finite values.
Results may differ from the reference program's by a relative error of at most 0.0062.
Values may be sent and summed in bfloat16 or wider, within the bound.
A program may use at most 128 MiB of HBM per device.

```python
import math
import jax
import jax.numpy as jnp
from jax import lax

NO = 12
NBR = 4
NW = 48
ATOM_DEV = 384
NE = 8
ATOMS = 1536
N_LAYER = 4


def draw_green_blocks(key, part):
    values = jax.random.truncated_normal(key, -3.0, 3.0, (NE, NO, NO, ATOMS), jnp.float32)
    symmetric = (values + jnp.swapaxes(values, 1, 2)) * 0.70710678
    return symmetric.astype(jnp.bfloat16)


def draw_neighbours(key, part):
    keys = jax.random.split(jax.random.fold_in(key, 11), 3)
    before = jax.random.randint(keys[0], (1, ATOMS), 0, ATOM_DEV, dtype=jnp.int32)
    after = jax.random.randint(keys[1], (1, ATOMS), 2 * ATOM_DEV, 3 * ATOM_DEV, dtype=jnp.int32)
    offsets = jax.random.randint(keys[2], (NBR - 2, ATOMS), 1, ATOM_DEV, dtype=jnp.int32)
    places = jnp.arange(ATOMS, dtype=jnp.int32) % ATOM_DEV
    inside = ATOM_DEV + (places[None, :] + offsets) % ATOM_DEV
    result = jnp.concatenate([before, after, inside], axis=0)
    result = result.at[0, 0].set(0)
    result = result.at[1, ATOMS - 1].set(3 * ATOM_DEV - 1)
    return result


def draw_phonon_shifts(key, part):
    largest = NE // 4
    values = jax.random.randint(jax.random.fold_in(key, 23), (NW,), 1, largest + 1, dtype=jnp.int32)
    values = values.at[0].set(1)
    values = values.at[1].set(largest)
    return values


def levels(key, extent, shards, low, top_value):
    gain, own = 1.0, jax.random.fold_in(key, 6)
    for dim, parts in shards:
        draws = jnp.exp(jax.random.uniform(jax.random.fold_in(own, dim), (parts,), jnp.float32, low / len(shards), top_value / len(shards)))
        gain = gain * jnp.repeat(draws, extent[dim] // parts).reshape([-1 if axis == dim else 1 for axis in range(len(extent))])
    return gain


def noise(stream_key, dims, spread, most, cuts=(), kind=jnp.bfloat16):
    array = spread * jax.random.normal(stream_key, dims, jnp.float32)
    if cuts:
        array = array * levels(stream_key, dims, cuts, -0.22, 0.18)
    return jnp.clip(array, -most, most).astype(kind)


def setup_inputs(seed: int = 0) -> dict:
    key_of = jax.random.split(jax.random.key(seed), 6)
    return {
        "green_blocks": draw_green_blocks(jax.random.fold_in(key_of[5], 71), 0),
        "coupling": noise(key_of[1], (NO, NO, NBR, ATOMS), NO ** -0.5, 1.75, ((3, 4),)),
        "phonon_weights": jnp.clip(jnp.exp(math.log(0.01) - 2.30258502 * jax.random.uniform(key_of[2], (2, NW, NBR, ATOMS), jnp.float32) ** levels(key_of[2], (2, NW, NBR, ATOMS), ((3, 4),), -0.2, 0.2)), 0.001, 0.01),
        "neighbours": draw_neighbours(jax.random.fold_in(key_of[5], 71), 0),
        "phonon_shifts": draw_phonon_shifts(jax.random.fold_in(key_of[5], 71), 0),
    }


def shift_tables(phonon_shifts, energy_count):
    energies = jnp.arange(energy_count, dtype=jnp.int32)
    target = energies[None, :, None]
    source = energies[None, None, :]
    offsets = phonon_shifts[:, None, None]
    lower_table = (source == target - offsets).astype(jnp.float32)
    upper_table = (source == target + offsets).astype(jnp.float32)
    return (lower_table, upper_table)

def reference(green_blocks, coupling, phonon_weights, neighbours, phonon_shifts):
    highest = lax.Precision.HIGHEST
    lower_table, upper_table = shift_tables(phonon_shifts, NE)
    padded = jnp.pad(green_blocks, ((0, 0), (0, 0), (0, 0), (ATOM_DEV, ATOM_DEV)))
    norm_factor = 1.0 / (NO * math.sqrt(NE))

    def one_slab(layer_index):
        atom_start = (layer_index * ATOM_DEV).astype(jnp.int32)
        window = lax.dynamic_slice_in_dim(padded, atom_start, 3 * ATOM_DEV, 3)
        slab_green = lax.dynamic_slice_in_dim(green_blocks, atom_start, ATOM_DEV, 3).astype(jnp.float32)
        slab_coupling = lax.dynamic_slice_in_dim(coupling, atom_start, ATOM_DEV, 3).astype(jnp.float32)
        slab_weights = lax.dynamic_slice_in_dim(phonon_weights, atom_start, ATOM_DEV, 3)
        slab_neighbours = lax.dynamic_slice_in_dim(neighbours, atom_start, ATOM_DEV, 1)
        gathered = jnp.take(window, slab_neighbours, axis=3).astype(jnp.float32)
        first_product = jnp.einsum('ipka,epqka->eiqka', slab_coupling, gathered, precision=highest)
        product = jnp.einsum('eiqka,jqka->eijka', first_product, slab_coupling, precision=highest).astype(jnp.bfloat16)
        product_wide = product.astype(jnp.float32)
        kernel = jnp.einsum('wka,wef->akef', slab_weights[0], lower_table, precision=highest)
        kernel = kernel + jnp.einsum('wka,wef->akef', slab_weights[1], upper_table, precision=highest)
        self_energy = jnp.einsum('akef,fijka->eija', kernel, product_wide, precision=highest).astype(jnp.bfloat16)
        correlation = jnp.einsum('fijka,eija->akfe', product_wide, slab_green, precision=highest)
        polarization = jnp.einsum('wef,akfe->wka', upper_table, correlation, precision=highest) * norm_factor
        left_product = jnp.einsum('eipa,epja->eija', slab_green, self_energy.astype(jnp.float32), precision=highest).astype(jnp.bfloat16)
        corrected = slab_green + jnp.einsum('eipa,epja->eija', left_product.astype(jnp.float32), slab_green, precision=highest)
        return (corrected.astype(jnp.bfloat16), polarization)
    corrected, polarization = lax.map(one_slab, jnp.arange(N_LAYER, dtype=jnp.int32))
    corrected = jnp.moveaxis(corrected, 0, 3).reshape(NE, NO, NO, ATOMS)
    polarization = jnp.moveaxis(polarization, 0, 2).reshape(NW, NBR, ATOMS)
    return (corrected, polarization)
```

```python
import functools
import math

import jax
import jax.numpy as jnp
import numpy as np
from jax import lax
from jax.experimental import pallas as pl
from jax.experimental.pallas import tpu as pltpu
from jax.sharding import PartitionSpec as P

MESH = pl.DeviceIdType.MESH
LANES = 128
F32 = jnp.float32
BF16 = jnp.bfloat16


def offsets(order):
    return [p * order - p * (p - 1) // 2 for p in range(order)]


def expansion(order, row_stride, packed_rows):
    off = offsets(order)
    table = np.zeros((order * row_stride, packed_rows), np.float32)
    for p in range(order):
        for q in range(order):
            low, high = min(p, q), max(p, q)
            table[p * row_stride + q, off[low] + high - low] = 1.0
    return jnp.asarray(table, BF16)


def kernel(
    reach, shift_ref, green_ref, coup_ref, weight_ref, near_ref, e12_ref, e16_ref,
    out_ref, pol_ref,
    tri32, own, halo, gin, pout, pin, chunks, cin, c4, g3, pscr, g16, s16, l16, ab,
    halo_send, halo_recv, gin_send, gin_recv, part_send, part_recv, chunk_send, chunk_recv,
):
    order = green_ref.shape[0]
    atoms = green_ref.shape[2]
    nbr = near_ref.shape[0]
    freqs = shift_ref.shape[0]
    tiles = atoms // LANES
    packed = own.shape[0]
    pad = c4.shape[2]
    ne = lax.axis_size("energy")
    nl = lax.axis_size("layer")
    me = lax.axis_index("energy")
    layer = lax.axis_index("layer")
    share = atoms // ne
    off = offsets(order)

    barrier = pltpu.get_barrier_semaphore()
    for r in range(1, ne):
        pl.semaphore_signal(
            barrier, inc=1, device_id={"energy": lax.rem(me + r, ne), "layer": layer},
            device_id_type=MESH,
        )

    @pl.when(layer > 0)
    def _():
        pl.semaphore_signal(
            barrier, inc=1, device_id={"energy": me, "layer": layer - 1}, device_id_type=MESH
        )

    @pl.when(layer < nl - 1)
    def _():
        pl.semaphore_signal(
            barrier, inc=1, device_id={"energy": me, "layer": layer + 1}, device_id_type=MESH
        )

    tri32[...] = jnp.zeros_like(tri32)
    for p in range(order):
        tri32[off[p] : off[p] + order - p, :] = green_ref[p].astype(F32)[p:, :]
    own[...] = tri32[...].astype(BF16)

    @pl.when(layer == 0)
    def _():
        halo[0] = jnp.zeros((packed, atoms), BF16)

    @pl.when(layer == nl - 1)
    def _():
        halo[1] = jnp.zeros((packed, atoms), BF16)

    for d in range(1, reach + 1):

        @pl.when(me < d)
        def _():
            gin[d - 1] = jnp.zeros((packed, atoms), BF16)
            pin[2 * d - 2] = jnp.zeros((packed, atoms), BF16)

        @pl.when(me + d >= ne)
        def _():
            pin[2 * d - 1] = jnp.zeros((packed, atoms), BF16)

    pl.semaphore_wait(
        barrier, ne - 1 + (layer > 0).astype(jnp.int32) + (layer < nl - 1).astype(jnp.int32)
    )

    def remote(src, dst, send, recv, energy, row):
        return pltpu.make_async_remote_copy(
            src_ref=src, dst_ref=dst, send_sem=send, recv_sem=recv,
            device_id={"energy": energy, "layer": row}, device_id_type=MESH,
        )

    def halo_copy(side):
        row = layer + 1 if side == 0 else layer - 1
        return remote(own, halo.at[side], halo_send.at[side], halo_recv.at[side], me, row)

    def green_copy(d):
        return remote(
            own, gin.at[d - 1], gin_send.at[d - 1], gin_recv.at[d - 1], me + d, layer
        )

    def part_copy(slot, energy):
        return remote(
            pout.at[slot], pin.at[slot], part_send.at[slot], part_recv.at[slot], energy, layer
        )

    def chunk_copy(r):
        dest = lax.rem(me + r, ne)
        return remote(
            chunks.at[dest], cin.at[r], chunk_send.at[r], chunk_recv.at[r], dest, layer
        )

    has_above, has_below = layer < nl - 1, layer > 0

    @pl.when(has_above)
    def _():
        halo_copy(0).start()

    @pl.when(has_below)
    def _():
        halo_copy(1).start()

    for d in range(1, reach + 1):

        @pl.when(me + d < ne)
        def _():
            green_copy(d).start()

    for t in range(tiles):
        block = coup_ref[:, :, t * LANES : (t + 1) * LANES].astype(F32)
        c4[:, :, t * nbr : (t + 1) * nbr, :] = block.reshape(order, order, nbr, LANES)

    def add_weights(w, sums):
        shift = shift_ref[w]
        low, high = weight_ref[w], weight_ref[freqs + w]
        new = []
        for d in range(1, reach + 1):
            pick = jnp.where(shift == d, 1.0, 0.0).astype(F32)
            new += [sums[2 * d - 2] + pick * low, sums[2 * d - 1] + pick * high]
        return tuple(new)

    sums = lax.fori_loop(
        0, freqs, add_weights, tuple(jnp.zeros((nbr, atoms), F32) for _ in range(2 * reach))
    )
    for s in range(2 * reach):
        ab[s] = sums[s]

    row = lax.broadcasted_iota(jnp.int32, (atoms, atoms), 0)

    def pick_neighbours(k, block, start):
        hot = jnp.where(row == near_ref[k : k + 1, :] - start, 1.0, 0.0).astype(BF16)
        full = jnp.dot(e12_ref[...], block, preferred_element_type=F32).astype(BF16)
        found = jnp.dot(full, hot, preferred_element_type=F32)
        for t in range(tiles):
            g3[pl.ds(t * nbr + k, order * order, stride=pad), :] = found[
                :, t * LANES : (t + 1) * LANES
            ]

    for k in range(2, nbr):
        pick_neighbours(k, own[...], atoms)

    g16[...] = jnp.dot(e16_ref[...], own[...], preferred_element_type=F32).reshape(g16.shape)

    @pl.when(has_below)
    def _():
        halo_copy(0).wait_recv()

    @pl.when(has_above)
    def _():
        halo_copy(1).wait_recv()

    pick_neighbours(0, halo[0], 0)
    pick_neighbours(1, halo[1], 2 * atoms)

    last = off[-1] + 1
    pscr[last * pad :, :] = jnp.zeros(((packed - last) * pad, LANES), F32)
    for i in range(order):
        first = jnp.zeros((order, pad, LANES), F32)
        for p in range(order):
            block = g3[p * order * pad : (p + 1) * order * pad, :].reshape(order, pad, LANES)
            first = first + c4[i, p][None] * block
        total = first[0][None] * c4[i:, 0]
        for q in range(1, order):
            total = total + first[q][None] * c4[i:, q]
        total = total.astype(BF16).astype(F32)
        pscr[off[i] * pad : (off[i] + order - i) * pad, :] = total.reshape(-1, LANES)

    for d in range(1, reach + 1):

        @pl.when(me >= d)
        def _():
            green_copy(d).wait_recv()

    index = lax.broadcasted_iota(jnp.int32, (packed, LANES), 0)
    twice = jnp.full((packed, LANES), 2.0, F32)
    for p in range(order):
        twice = jnp.where(index == off[p], 1.0, twice)
    rows = [[] for _ in range(reach * nbr)]
    for t in range(tiles):
        lanes = slice(t * LANES, (t + 1) * LANES)
        greens = [gin[d, :, lanes].astype(F32) * twice for d in range(reach)]
        parts = [None] * (2 * reach)
        for k in range(nbr):
            value = pscr[pl.ds(t * nbr + k, packed, stride=pad), :]
            for s in range(2 * reach):
                term = ab[s, k : k + 1, lanes] * value
                parts[s] = term if parts[s] is None else parts[s] + term
            for d in range(reach):
                rows[d * nbr + k].append(jnp.sum(greens[d] * value, axis=0, keepdims=True))
        for s in range(2 * reach):
            pout[s, :, lanes] = parts[s].astype(BF16)

    for d in range(1, reach + 1):

        @pl.when(me + d < ne)
        def _():
            part_copy(2 * d - 2, me + d).start()

        @pl.when(me >= d)
        def _():
            part_copy(2 * d - 1, me - d).start()

    corr = jnp.concatenate([jnp.concatenate(r, axis=1) for r in rows], axis=0)
    width = chunks.shape[2]
    for e in range(ne):
        moved = corr if e == 0 else pltpu.roll(corr, atoms - e * share, 1)
        chunks[e] = moved[:, :width]
    for r in range(1, ne):
        chunk_copy(r).start()

    for d in range(1, reach + 1):

        @pl.when(me >= d)
        def _():
            part_copy(2 * d - 2, me).wait_recv()

        @pl.when(me + d < ne)
        def _():
            part_copy(2 * d - 1, me).wait_recv()

    sigma = pin[0].astype(F32)
    for s in range(1, 2 * reach):
        sigma = sigma + pin[s].astype(F32)
    s16[...] = jnp.dot(
        e16_ref[...], sigma.astype(BF16), preferred_element_type=F32
    ).reshape(s16.shape)

    def dyson(i, carry):
        left = g16[i, 0:1, :] * s16[0]
        for p in range(1, order):
            left = left + g16[i, p : p + 1, :] * s16[p]
        l16[...] = left.astype(BF16).astype(F32)
        total = g16[i]
        for p in range(order):
            total = total + l16[p : p + 1, :] * g16[p]
        out_ref[i] = total[:order].astype(BF16)
        return carry

    lax.fori_loop(0, order, dyson, 0)

    for r in range(1, ne):
        chunk_copy(r).wait_recv()
    summed = chunks[me]
    for r in range(1, ne):
        summed = summed + cin[r]
    summed = summed * (1.0 / (order * math.sqrt(ne)))
    summed = summed[:, :share]

    def expand(w, carry):
        shift = shift_ref[w]
        value = jnp.zeros((nbr, share), F32)
        for d in range(1, reach + 1):
            pick = jnp.where(shift == d, 1.0, 0.0).astype(F32)
            value = value + pick * summed[(d - 1) * nbr : d * nbr]
        pol_ref[w] = value
        return carry

    lax.fori_loop(0, freqs, expand, 0)

    @pl.when(has_above)
    def _():
        halo_copy(0).wait_send()

    @pl.when(has_below)
    def _():
        halo_copy(1).wait_send()

    for d in range(1, reach + 1):

        @pl.when(me + d < ne)
        def _():
            green_copy(d).wait_send()
            part_copy(2 * d - 2, me).wait_send()

        @pl.when(me >= d)
        def _():
            part_copy(2 * d - 1, me).wait_send()

    for r in range(1, ne):
        chunk_copy(r).wait_send()


def body(green_blocks, coupling, phonon_weights, neighbours, phonon_shifts):
    ne = lax.axis_size("energy")
    reach = max(ne // 4, 1)
    order = green_blocks.shape[1]
    atoms = green_blocks.shape[3]
    nbr = neighbours.shape[0]
    freqs = phonon_shifts.shape[0]
    tiles = atoms // LANES
    share = atoms // ne
    count = order * (order + 1) // 2
    packed = -(-count // 16) * 16
    pad = -(-(tiles * nbr) // 8) * 8
    rows = 16 * (-(-order // 16))
    width = -(-share // LANES) * LANES
    vmem = pl.BlockSpec(memory_space=pltpu.VMEM)
    smem = pl.BlockSpec(memory_space=pltpu.SMEM)
    dma = pltpu.SemaphoreType.DMA
    corrected, polarization = pl.pallas_call(
        functools.partial(kernel, reach),
        out_shape=(
            jax.ShapeDtypeStruct((order, order, atoms), BF16),
            jax.ShapeDtypeStruct((freqs, nbr, share), F32),
        ),
        in_specs=[smem, vmem, vmem, vmem, vmem, vmem, vmem],
        out_specs=(vmem, vmem),
        scratch_shapes=[
            pltpu.VMEM((packed, atoms), F32),
            pltpu.VMEM((packed, atoms), BF16),
            pltpu.VMEM((2, packed, atoms), BF16),
            pltpu.VMEM((reach, packed, atoms), BF16),
            pltpu.VMEM((2 * reach, packed, atoms), BF16),
            pltpu.VMEM((2 * reach, packed, atoms), BF16),
            pltpu.VMEM((ne, reach * nbr, width), F32),
            pltpu.VMEM((ne, reach * nbr, width), F32),
            pltpu.VMEM((order, order, pad, LANES), F32),
            pltpu.VMEM((order * order * pad, LANES), F32),
            pltpu.VMEM((packed * pad, LANES), F32),
            pltpu.VMEM((order, rows, atoms), F32),
            pltpu.VMEM((order, rows, atoms), F32),
            pltpu.VMEM((rows, atoms), F32),
            pltpu.VMEM((2 * reach, nbr, atoms), F32),
            dma((2,)), dma((2,)), dma((reach,)), dma((reach,)),
            dma((2 * reach,)), dma((2 * reach,)), dma((ne,)), dma((ne,)),
        ],
        compiler_params=pltpu.CompilerParams(collective_id=0, has_side_effects=True),
    )(
        phonon_shifts,
        green_blocks[0],
        coupling.reshape(order * order, nbr, atoms),
        phonon_weights.reshape(2 * freqs, nbr, atoms),
        neighbours,
        expansion(order, order, packed),
        expansion(order, rows, packed),
    )
    return corrected[None], polarization


def solution(mesh):
    return jax.shard_map(
        body,
        mesh=mesh,
        in_specs=(
            P("energy", None, None, "layer"),
            P(None, None, None, "layer"),
            P(None, None, None, "layer"),
            P(None, "layer"),
            P(),
        ),
        out_specs=(P("energy", None, None, "layer"), P(None, None, ("layer", "energy"))),
        check_vma=False,
    )
```

```python
import functools
import math

import jax
import jax.numpy as jnp
import numpy as np
from jax import lax
from jax.experimental import pallas as pl
from jax.experimental.pallas import tpu as pltpu
from jax.sharding import PartitionSpec as P

MESH = pl.DeviceIdType.MESH
LANES = 128
F32 = jnp.float32
BF16 = jnp.bfloat16


def offsets(order):
    return [p * order - p * (p - 1) // 2 for p in range(order)]


def expansion(order, row_stride, packed_rows):
    off = offsets(order)
    table = np.zeros((order * row_stride, packed_rows), np.float32)
    for p in range(order):
        for q in range(order):
            low, high = min(p, q), max(p, q)
            table[p * row_stride + q, off[low] + high - low] = 1.0
    return jnp.asarray(table, BF16)


def kernel(
    reach, shift_ref, green_ref, coup_hbm, weight_hbm, near_ref, e12_ref,
    sig_ref, sum_ref,
    coup_ref, weight_ref, tri32, own, halo, gin, pout, pin, pacc, chunks, cin, c4, g3, pscr, ab,
    load_sem, halo_send, halo_recv, gin_send, gin_recv, part_send, part_recv,
    chunk_send, chunk_recv,
):
    order = green_ref.shape[0]
    atoms = green_ref.shape[2]
    nbr = near_ref.shape[0]
    freqs = shift_ref.shape[0]
    tiles = atoms // LANES
    packed = own.shape[0]
    pad = c4.shape[3]
    ne = lax.axis_size("energy")
    nl = lax.axis_size("layer")
    me = lax.axis_index("energy")
    layer = lax.axis_index("layer")
    share = atoms // ne
    off = offsets(order)
    groups = (tuple(range(2, nbr)), (0, 1))

    load_coup = pltpu.make_async_copy(coup_hbm, coup_ref, load_sem.at[0])
    load_weight = pltpu.make_async_copy(weight_hbm, weight_ref, load_sem.at[1])
    load_coup.start()
    load_weight.start()

    barrier = pltpu.get_barrier_semaphore()
    for r in range(1, ne):
        pl.semaphore_signal(
            barrier, inc=1, device_id={"energy": lax.rem(me + r, ne), "layer": layer},
            device_id_type=MESH,
        )

    @pl.when(layer > 0)
    def _():
        pl.semaphore_signal(
            barrier, inc=1, device_id={"energy": me, "layer": layer - 1}, device_id_type=MESH
        )

    @pl.when(layer < nl - 1)
    def _():
        pl.semaphore_signal(
            barrier, inc=1, device_id={"energy": me, "layer": layer + 1}, device_id_type=MESH
        )

    tri32[...] = jnp.zeros_like(tri32)
    for p in range(order):
        tri32[off[p] : off[p] + order - p, :] = green_ref[p].astype(F32)[p:, :]
    own[...] = tri32[...].astype(BF16)

    @pl.when(layer == 0)
    def _():
        halo[0] = jnp.zeros((packed, atoms), BF16)

    @pl.when(layer == nl - 1)
    def _():
        halo[1] = jnp.zeros((packed, atoms), BF16)

    for d in range(1, reach + 1):

        @pl.when(me < d)
        def _():
            gin[d - 1] = jnp.zeros((packed, atoms), BF16)
            pin[2 * d - 2] = jnp.zeros((packed, atoms), BF16)

        @pl.when(me + d >= ne)
        def _():
            pin[2 * d - 1] = jnp.zeros((packed, atoms), BF16)

    pl.semaphore_wait(
        barrier, ne - 1 + (layer > 0).astype(jnp.int32) + (layer < nl - 1).astype(jnp.int32)
    )

    def remote(src, dst, send, recv, energy, row):
        return pltpu.make_async_remote_copy(
            src_ref=src, dst_ref=dst, send_sem=send, recv_sem=recv,
            device_id={"energy": energy, "layer": row}, device_id_type=MESH,
        )

    def halo_copy(side):
        row = layer + 1 if side == 0 else layer - 1
        return remote(own, halo.at[side], halo_send.at[side], halo_recv.at[side], me, row)

    def green_copy(d):
        return remote(
            own, gin.at[d - 1], gin_send.at[d - 1], gin_recv.at[d - 1], me + d, layer
        )

    def part_copy(slot, energy):
        return remote(
            pout.at[slot], pin.at[slot], part_send.at[slot], part_recv.at[slot], energy, layer
        )

    def chunk_copy(r):
        dest = lax.rem(me + r, ne)
        return remote(
            chunks.at[dest], cin.at[r], chunk_send.at[r], chunk_recv.at[r], dest, layer
        )

    has_above, has_below = layer < nl - 1, layer > 0

    @pl.when(has_above)
    def _():
        halo_copy(0).start()

    @pl.when(has_below)
    def _():
        halo_copy(1).start()

    for d in range(1, reach + 1):

        @pl.when(me + d < ne)
        def _():
            green_copy(d).start()

    row = lax.broadcasted_iota(jnp.int32, (atoms, atoms), 0)

    def pick_neighbours(g, j, full, start):
        k, size = groups[g][j], len(groups[g])
        hot = jnp.where(row == near_ref[k : k + 1, :] - start, 1.0, 0.0).astype(BF16)
        found = jnp.dot(full, hot, preferred_element_type=F32)
        for t in range(tiles):
            g3[pl.ds(t * size + j, order * order, stride=pad), :] = found[
                :, t * LANES : (t + 1) * LANES
            ]

    def expanded(block):
        return jnp.dot(e12_ref[...], block, preferred_element_type=F32).astype(BF16)

    own_full = expanded(own[...])
    for j in range(len(groups[0])):
        pick_neighbours(0, j, own_full, atoms)

    load_coup.wait()
    for g, slots in enumerate(groups):
        size = len(slots)
        for t in range(tiles):
            block = coup_ref[:, :, t * LANES : (t + 1) * LANES].astype(F32)
            block = block.reshape(order, order, nbr, LANES)
            c4[g, :, :, t * size : (t + 1) * size, :] = block[
                :, :, slots[0] : slots[0] + size, :
            ]

    last = off[-1] + 1
    for g in range(2):
        pscr[g, last * pad :, :] = jnp.zeros(((packed - last) * pad, LANES), F32)

    def products(g):
        for i in range(0, order, 2):
            first = jnp.zeros((2, order, pad, LANES), F32)
            for p in range(order):
                block = g3[p * order * pad : (p + 1) * order * pad, :]
                block = block.reshape(order, pad, LANES)
                first = first + c4[g, i : i + 2, p][:, None] * block[None]
            total = first[:, 0][:, None] * c4[g, i:, 0][None]
            for q in range(1, order):
                total = total + first[:, q][:, None] * c4[g, i:, q][None]
            total = total.astype(BF16).astype(F32)
            for n in range(2):
                pscr[g, off[i + n] * pad : (off[i + n] + order - i - n) * pad, :] = total[
                    n, n:
                ].reshape(-1, LANES)

    products(0)

    load_weight.wait()

    def add_weights(w, sums):
        shift = shift_ref[w]
        low, high = weight_ref[w], weight_ref[freqs + w]
        new = []
        for d in range(1, reach + 1):
            pick = jnp.where(shift == d, 1.0, 0.0).astype(F32)
            new += [sums[2 * d - 2] + pick * low, sums[2 * d - 1] + pick * high]
        return tuple(new)

    sums = lax.fori_loop(
        0, freqs, add_weights, tuple(jnp.zeros((nbr, atoms), F32) for _ in range(2 * reach)),
        unroll=4,
    )
    for s in range(2 * reach):
        ab[s] = sums[s]

    def partials(g, t, s):
        slots, lanes = groups[g], slice(t * LANES, (t + 1) * LANES)
        total = None
        for j, k in enumerate(slots):
            value = pscr[g, pl.ds(t * len(slots) + j, packed, stride=pad), :]
            term = ab[s, k : k + 1, lanes] * value
            total = term if total is None else total + term
        return total

    for t in range(tiles):
        for s in range(2 * reach):
            pacc[s, :, t * LANES : (t + 1) * LANES] = partials(0, t, s)

    @pl.when(has_below)
    def _():
        halo_copy(0).wait_recv()

    @pl.when(has_above)
    def _():
        halo_copy(1).wait_recv()

    pick_neighbours(1, 0, expanded(halo[0]), 0)
    pick_neighbours(1, 1, expanded(halo[1]), 2 * atoms)
    products(1)

    for t in range(tiles):
        lanes = slice(t * LANES, (t + 1) * LANES)
        for s in range(2 * reach):
            pout[s, :, lanes] = (pacc[s, :, lanes] + partials(1, t, s)).astype(BF16)

    for d in range(1, reach + 1):

        @pl.when(me + d < ne)
        def _():
            part_copy(2 * d - 2, me + d).start()

        @pl.when(me >= d)
        def _():
            part_copy(2 * d - 1, me - d).start()

    for d in range(1, reach + 1):

        @pl.when(me >= d)
        def _():
            green_copy(d).wait_recv()

    index = lax.broadcasted_iota(jnp.int32, (packed, LANES), 0)
    twice = jnp.full((packed, LANES), 2.0, F32)
    for p in range(order):
        twice = jnp.where(index == off[p], 1.0, twice)
    rows = [[] for _ in range(reach * nbr)]
    for t in range(tiles):
        lanes = slice(t * LANES, (t + 1) * LANES)
        greens = [gin[d, :, lanes].astype(F32) * twice for d in range(reach)]
        for g, slots in enumerate(groups):
            for j, k in enumerate(slots):
                value = pscr[g, pl.ds(t * len(slots) + j, packed, stride=pad), :]
                for d in range(reach):
                    rows[d * nbr + k].append(jnp.sum(greens[d] * value, axis=0, keepdims=True))

    corr = jnp.concatenate([jnp.concatenate(r, axis=1) for r in rows], axis=0)
    width = chunks.shape[2]
    for e in range(ne):
        moved = corr if e == 0 else pltpu.roll(corr, atoms - e * share, 1)
        chunks[e] = moved[:, :width]
    for r in range(1, ne):
        chunk_copy(r).start()

    for d in range(1, reach + 1):

        @pl.when(me >= d)
        def _():
            part_copy(2 * d - 2, me).wait_recv()

        @pl.when(me + d < ne)
        def _():
            part_copy(2 * d - 1, me).wait_recv()

    sigma = pin[0].astype(F32)
    for s in range(1, 2 * reach):
        sigma = sigma + pin[s].astype(F32)
    sig_ref[...] = sigma.astype(BF16)

    for r in range(1, ne):
        chunk_copy(r).wait_recv()
    summed = chunks[me]
    for r in range(1, ne):
        summed = summed + cin[r]
    sum_ref[...] = summed * (1.0 / (order * math.sqrt(ne)))

    @pl.when(has_above)
    def _():
        halo_copy(0).wait_send()

    @pl.when(has_below)
    def _():
        halo_copy(1).wait_send()

    for d in range(1, reach + 1):

        @pl.when(me + d < ne)
        def _():
            green_copy(d).wait_send()
            part_copy(2 * d - 2, me).wait_send()

        @pl.when(me >= d)
        def _():
            part_copy(2 * d - 1, me).wait_send()

    for r in range(1, ne):
        chunk_copy(r).wait_send()


def finish(
    reach, shift_ref, green_ref, sig_ref, sum_ref, e16_ref, out_ref, pol_ref, g16, s16, l16
):
    order = green_ref.shape[0]
    nbr, share = pol_ref.shape[1:]
    freqs = shift_ref.shape[0]
    rows = g16.shape[1]
    s16[...] = jnp.dot(
        e16_ref[...], sig_ref[...], preferred_element_type=F32
    ).reshape(s16.shape)
    g16[...] = jnp.zeros_like(g16)
    for p in range(order):
        g16[p, :order, :] = green_ref[p].astype(F32)

    for i in range(0, order, 2):
        left = [g16[i + n, 0:1, :] * s16[0] for n in range(2)]
        for p in range(1, order):
            block = s16[p]
            left = [left[n] + g16[i + n, p : p + 1, :] * block for n in range(2)]
        for n in range(2):
            l16[i + n] = left[n].astype(BF16).astype(F32)
    for i in range(0, order, 2):
        total = [g16[i + n] for n in range(2)]
        for p in range(order):
            block = g16[p]
            total = [total[n] + l16[i + n, p : p + 1, :] * block for n in range(2)]
        for n in range(2):
            out_ref[i + n] = total[n][:order].astype(BF16)

    summed = sum_ref[:, :share]
    for w in range(freqs):
        shift = shift_ref[w]
        value = jnp.zeros((nbr, share), F32)
        for d in range(1, reach + 1):
            value = jnp.where(shift == d, summed[(d - 1) * nbr : d * nbr], value)
        pol_ref[w] = value


def body(green_blocks, coupling, phonon_weights, neighbours, phonon_shifts):
    ne = lax.axis_size("energy")
    reach = max(ne // 4, 1)
    order = green_blocks.shape[1]
    atoms = green_blocks.shape[3]
    nbr = neighbours.shape[0]
    freqs = phonon_shifts.shape[0]
    tiles = atoms // LANES
    share = atoms // ne
    count = order * (order + 1) // 2
    packed = -(-count // 16) * 16
    pad = -(-(tiles * max(nbr - 2, 2)) // 8) * 8
    rows = 16 * (-(-order // 16))
    width = -(-share // LANES) * LANES
    vmem = pl.BlockSpec(memory_space=pltpu.VMEM)
    smem = pl.BlockSpec(memory_space=pltpu.SMEM)
    hbm = pl.BlockSpec(memory_space=pl.ANY)
    dma = pltpu.SemaphoreType.DMA
    green = green_blocks[0]
    sigma, summed = pl.pallas_call(
        functools.partial(kernel, reach),
        out_shape=(
            jax.ShapeDtypeStruct((packed, atoms), BF16),
            jax.ShapeDtypeStruct((reach * nbr, width), F32),
        ),
        in_specs=[smem, vmem, hbm, hbm, vmem, vmem],
        out_specs=(vmem, vmem),
        scratch_shapes=[
            pltpu.VMEM((order * order, nbr, atoms), BF16),
            pltpu.VMEM((2 * freqs, nbr, atoms), F32),
            pltpu.VMEM((packed, atoms), F32),
            pltpu.VMEM((packed, atoms), BF16),
            pltpu.VMEM((2, packed, atoms), BF16),
            pltpu.VMEM((reach, packed, atoms), BF16),
            pltpu.VMEM((2 * reach, packed, atoms), BF16),
            pltpu.VMEM((2 * reach, packed, atoms), BF16),
            pltpu.VMEM((2 * reach, packed, atoms), F32),
            pltpu.VMEM((ne, reach * nbr, width), F32),
            pltpu.VMEM((ne, reach * nbr, width), F32),
            pltpu.VMEM((2, order, order, pad, LANES), F32),
            pltpu.VMEM((order * order * pad, LANES), F32),
            pltpu.VMEM((2, packed * pad, LANES), F32),
            pltpu.VMEM((2 * reach, nbr, atoms), F32),
            dma((2,)), dma((2,)), dma((2,)), dma((reach,)), dma((reach,)),
            dma((2 * reach,)), dma((2 * reach,)), dma((ne,)), dma((ne,)),
        ],
        compiler_params=pltpu.CompilerParams(
            collective_id=0, has_side_effects=True, vmem_limit_bytes=32 << 20
        ),
    )(
        phonon_shifts,
        green,
        coupling.reshape(order * order, nbr, atoms),
        phonon_weights.reshape(2 * freqs, nbr, atoms),
        neighbours,
        expansion(order, order, packed),
    )
    corrected, polarization = pl.pallas_call(
        functools.partial(finish, reach),
        out_shape=(
            jax.ShapeDtypeStruct((order, order, atoms), BF16),
            jax.ShapeDtypeStruct((freqs, nbr, share), F32),
        ),
        in_specs=[smem, vmem, vmem, vmem, vmem],
        out_specs=(vmem, vmem),
        scratch_shapes=[pltpu.VMEM((order, rows, atoms), F32)] * 3,
        compiler_params=pltpu.CompilerParams(vmem_limit_bytes=32 << 20),
    )(phonon_shifts, green, sigma, summed, expansion(order, rows, packed))
    return corrected[None], polarization


def solution(mesh):
    return jax.shard_map(
        body,
        mesh=mesh,
        in_specs=(
            P("energy", None, None, "layer"),
            P(None, None, None, "layer"),
            P(None, None, None, "layer"),
            P(None, "layer"),
            P(),
        ),
        out_specs=(P("energy", None, None, "layer"), P(None, None, ("layer", "energy"))),
        check_vma=False,
    )
```

```python
import functools
import math

import jax
import jax.numpy as jnp
import numpy as np
from jax import lax
from jax.experimental import pallas as pl
from jax.experimental.pallas import tpu as pltpu
from jax.sharding import PartitionSpec as P

MESH = pl.DeviceIdType.MESH
LANES = 128
F32 = jnp.float32
BF16 = jnp.bfloat16


def offsets(order):
    return [p * order - p * (p - 1) // 2 for p in range(order)]


def expansion(order, row_stride, packed_rows):
    off = offsets(order)
    table = np.zeros((order * row_stride, packed_rows), np.float32)
    for p in range(order):
        for q in range(order):
            low, high = min(p, q), max(p, q)
            table[p * row_stride + q, off[low] + high - low] = 1.0
    return jnp.asarray(table, BF16)


def kernel(
    reach, shift_hbm, green_hbm, coup_hbm, weight_hbm, near_hbm, e12_hbm,
    sig_ref, sum_ref,
    shift_ref, green_ref, coup_ref, weight_ref, near_ref, e12_ref, tri32, own, halo, gin, pout, pin, pacc, chunks, cin, c4, g3, pscr, ab,
    load_sem, halo_send, halo_recv, gin_send, gin_recv, part_send, part_recv,
    chunk_send, chunk_recv,
):
    order = green_ref.shape[0]
    atoms = green_ref.shape[2]
    nbr = near_ref.shape[0]
    freqs = shift_ref.shape[0]
    tiles = atoms // LANES
    packed = own.shape[0]
    pad = c4.shape[3]
    ne = lax.axis_size("energy")
    nl = lax.axis_size("layer")
    me = lax.axis_index("energy")
    layer = lax.axis_index("layer")
    share = atoms // ne
    off = offsets(order)
    groups = (tuple(range(2, nbr)), (0, 1))

    def load(n, src, dst):
        copy = pltpu.make_async_copy(src, dst, load_sem.at[n])
        copy.start()
        return copy

    load_green = load(0, green_hbm, green_ref)
    load_near = load(1, near_hbm, near_ref)
    load_e12 = load(2, e12_hbm, e12_ref)
    load_coup = load(3, coup_hbm, coup_ref)
    load_weight = load(4, weight_hbm, weight_ref)
    load_shift = load(5, shift_hbm, shift_ref)

    barrier = pltpu.get_barrier_semaphore()
    for r in range(1, ne):
        pl.semaphore_signal(
            barrier, inc=1, device_id={"energy": lax.rem(me + r, ne), "layer": layer},
            device_id_type=MESH,
        )

    @pl.when(layer > 0)
    def _():
        pl.semaphore_signal(
            barrier, inc=1, device_id={"energy": me, "layer": layer - 1}, device_id_type=MESH
        )

    @pl.when(layer < nl - 1)
    def _():
        pl.semaphore_signal(
            barrier, inc=1, device_id={"energy": me, "layer": layer + 1}, device_id_type=MESH
        )

    tri32[...] = jnp.zeros_like(tri32)
    load_green.wait()
    for p in range(order):
        tri32[off[p] : off[p] + order - p, :] = green_ref[p].astype(F32)[p:, :]
    own[...] = tri32[...].astype(BF16)

    @pl.when(layer == 0)
    def _():
        halo[0] = jnp.zeros((packed, atoms), BF16)

    @pl.when(layer == nl - 1)
    def _():
        halo[1] = jnp.zeros((packed, atoms), BF16)

    for d in range(1, reach + 1):

        @pl.when(me < d)
        def _():
            gin[d - 1] = jnp.zeros((packed, atoms), BF16)
            pin[2 * d - 2] = jnp.zeros(pin.shape[1:], BF16)

        @pl.when(me + d >= ne)
        def _():
            pin[2 * d - 1] = jnp.zeros(pin.shape[1:], BF16)

    pl.semaphore_wait(
        barrier, ne - 1 + (layer > 0).astype(jnp.int32) + (layer < nl - 1).astype(jnp.int32)
    )

    def remote(src, dst, send, recv, energy, row):
        return pltpu.make_async_remote_copy(
            src_ref=src, dst_ref=dst, send_sem=send, recv_sem=recv,
            device_id={"energy": energy, "layer": row}, device_id_type=MESH,
        )

    def halo_copy(side):
        row = layer + 1 if side == 0 else layer - 1
        return remote(own, halo.at[side], halo_send.at[side], halo_recv.at[side], me, row)

    def green_copy(d):
        return remote(
            own, gin.at[d - 1], gin_send.at[d - 1], gin_recv.at[d - 1], me + d, layer
        )

    def part_copy(slot, t, energy):
        return remote(
            pout.at[slot, t], pin.at[slot, t], part_send.at[slot, t], part_recv.at[slot, t],
            energy, layer,
        )

    def chunk_copy(r):
        dest = lax.rem(me + r, ne)
        return remote(
            chunks.at[dest], cin.at[r], chunk_send.at[r], chunk_recv.at[r], dest, layer
        )

    has_above, has_below = layer < nl - 1, layer > 0

    @pl.when(has_above)
    def _():
        halo_copy(0).start()

    @pl.when(has_below)
    def _():
        halo_copy(1).start()

    for d in range(1, reach + 1):

        @pl.when(me + d < ne)
        def _():
            green_copy(d).start()

    row = lax.broadcasted_iota(jnp.int32, (atoms, atoms), 0)

    def pick_neighbours(g, j, full, start):
        k, size = groups[g][j], len(groups[g])
        hot = jnp.where(row == near_ref[k : k + 1, :] - start, 1.0, 0.0).astype(BF16)
        found = jnp.dot(full, hot, preferred_element_type=F32)
        for t in range(tiles):
            g3[pl.ds(t * size + j, order * order, stride=pad), :] = found[
                :, t * LANES : (t + 1) * LANES
            ]

    def expanded(block):
        return jnp.dot(e12_ref[...], block, preferred_element_type=F32).astype(BF16)

    load_near.wait()
    load_e12.wait()
    own_full = expanded(own[...])
    for j in range(len(groups[0])):
        pick_neighbours(0, j, own_full, atoms)

    load_coup.wait()
    for g, slots in enumerate(groups):
        size = len(slots)
        for t in range(tiles):
            block = coup_ref[:, :, t * LANES : (t + 1) * LANES].astype(F32)
            block = block.reshape(order, order, nbr, LANES)
            c4[g, :, :, t * size : (t + 1) * size, :] = block[
                :, :, slots[0] : slots[0] + size, :
            ]

    last = off[-1] + 1
    for g in range(2):
        pscr[g, last * pad :, :] = jnp.zeros(((packed - last) * pad, LANES), F32)

    def products(g):
        for i in range(0, order, 2):
            first = jnp.zeros((2, order, pad, LANES), F32)
            for p in range(order):
                block = g3[p * order * pad : (p + 1) * order * pad, :]
                block = block.reshape(order, pad, LANES)
                first = first + c4[g, i : i + 2, p][:, None] * block[None]
            total = first[:, 0][:, None] * c4[g, i:, 0][None]
            for q in range(1, order):
                total = total + first[:, q][:, None] * c4[g, i:, q][None]
            total = total.astype(BF16).astype(F32)
            for n in range(2):
                pscr[g, off[i + n] * pad : (off[i + n] + order - i - n) * pad, :] = total[
                    n, n:
                ].reshape(-1, LANES)

    products(0)

    load_weight.wait()
    load_shift.wait()

    def add_weights(w, sums):
        shift = shift_ref[w]
        low, high = weight_ref[w], weight_ref[freqs + w]
        new = []
        for d in range(1, reach + 1):
            pick = jnp.where(shift == d, 1.0, 0.0).astype(F32)
            new += [sums[2 * d - 2] + pick * low, sums[2 * d - 1] + pick * high]
        return tuple(new)

    sums = lax.fori_loop(
        0, freqs, add_weights, tuple(jnp.zeros((nbr, atoms), F32) for _ in range(2 * reach)),
        unroll=4,
    )
    for s in range(2 * reach):
        ab[s] = sums[s]

    def partials(g, t, s):
        slots, lanes = groups[g], slice(t * LANES, (t + 1) * LANES)
        total = None
        for j, k in enumerate(slots):
            value = pscr[g, pl.ds(t * len(slots) + j, packed, stride=pad), :]
            term = ab[s, k : k + 1, lanes] * value
            total = term if total is None else total + term
        return total

    for t in range(tiles):
        for s in range(2 * reach):
            pacc[s, t] = partials(0, t, s)

    for d in range(1, reach + 1):

        @pl.when(me >= d)
        def _():
            green_copy(d).wait_recv()

    index = lax.broadcasted_iota(jnp.int32, (packed, LANES), 0)
    twice = jnp.full((packed, LANES), 2.0, F32)
    for p in range(order):
        twice = jnp.where(index == off[p], 1.0, twice)
    rows = [[None] * tiles for _ in range(reach * nbr)]

    def correlate(g):
        slots = groups[g]
        for t in range(tiles):
            lanes = slice(t * LANES, (t + 1) * LANES)
            greens = [gin[d, :, lanes].astype(F32) * twice for d in range(reach)]
            for j, k in enumerate(slots):
                value = pscr[g, pl.ds(t * len(slots) + j, packed, stride=pad), :]
                for d in range(reach):
                    rows[d * nbr + k][t] = jnp.sum(greens[d] * value, axis=0, keepdims=True)

    correlate(0)

    @pl.when(has_below)
    def _():
        halo_copy(0).wait_recv()

    @pl.when(has_above)
    def _():
        halo_copy(1).wait_recv()

    pick_neighbours(1, 0, expanded(halo[0]), 0)
    pick_neighbours(1, 1, expanded(halo[1]), 2 * atoms)
    products(1)

    correlate(1)
    corr = jnp.concatenate([jnp.concatenate(r, axis=1) for r in rows], axis=0)
    width = chunks.shape[2]
    for e in range(ne):
        moved = corr if e == 0 else pltpu.roll(corr, atoms - e * share, 1)
        chunks[e] = moved[:, :width]
    for r in range(1, ne):
        chunk_copy(r).start()

    for t in range(tiles):
        for s in range(2 * reach):
            pout[s, t] = (pacc[s, t] + partials(1, t, s)).astype(BF16)
        for d in range(1, reach + 1):

            @pl.when(me + d < ne)
            def _():
                part_copy(2 * d - 2, t, me + d).start()

            @pl.when(me >= d)
            def _():
                part_copy(2 * d - 1, t, me - d).start()

    for t in range(tiles):
        for d in range(1, reach + 1):

            @pl.when(me >= d)
            def _():
                part_copy(2 * d - 2, t, me).wait_recv()

            @pl.when(me + d < ne)
            def _():
                part_copy(2 * d - 1, t, me).wait_recv()

        sigma = pin[0, t].astype(F32)
        for s in range(1, 2 * reach):
            sigma = sigma + pin[s, t].astype(F32)
        sig_ref[:, t * LANES : (t + 1) * LANES] = sigma.astype(BF16)

    for r in range(1, ne):
        chunk_copy(r).wait_recv()
    summed = chunks[me]
    for r in range(1, ne):
        summed = summed + cin[r]
    sum_ref[...] = summed * (1.0 / (order * math.sqrt(ne)))

    @pl.when(has_above)
    def _():
        halo_copy(0).wait_send()

    @pl.when(has_below)
    def _():
        halo_copy(1).wait_send()

    for d in range(1, reach + 1):

        @pl.when(me + d < ne)
        def _():
            green_copy(d).wait_send()
            for t in range(tiles):
                part_copy(2 * d - 2, t, me).wait_send()

        @pl.when(me >= d)
        def _():
            for t in range(tiles):
                part_copy(2 * d - 1, t, me).wait_send()

    for r in range(1, ne):
        chunk_copy(r).wait_send()


def finish(
    reach, shift_ref, green_ref, sig_ref, sum_ref, e16_ref, out_ref, pol_ref, g16, s16, l16
):
    order = green_ref.shape[0]
    nbr, share = pol_ref.shape[1:]
    freqs = shift_ref.shape[0]
    rows = g16.shape[1]
    s16[...] = jnp.dot(
        e16_ref[...], sig_ref[...], preferred_element_type=F32
    ).reshape(s16.shape)
    g16[...] = jnp.zeros_like(g16)
    for p in range(order):
        g16[p, :order, :] = green_ref[p].astype(F32)

    for i in range(0, order, 2):
        left = [g16[i + n, 0:1, :] * s16[0] for n in range(2)]
        for p in range(1, order):
            block = s16[p]
            left = [left[n] + g16[i + n, p : p + 1, :] * block for n in range(2)]
        for n in range(2):
            l16[i + n] = left[n].astype(BF16).astype(F32)
    for i in range(0, order, 2):
        total = [g16[i + n] for n in range(2)]
        for p in range(order):
            block = g16[p]
            total = [total[n] + l16[i + n, p : p + 1, :] * block for n in range(2)]
        for n in range(2):
            out_ref[i + n] = total[n][:order].astype(BF16)

    summed = sum_ref[:, :share]
    for w in range(freqs):
        shift = shift_ref[w]
        value = jnp.zeros((nbr, share), F32)
        for d in range(1, reach + 1):
            value = jnp.where(shift == d, summed[(d - 1) * nbr : d * nbr], value)
        pol_ref[w] = value


def body(green_blocks, coupling, phonon_weights, neighbours, phonon_shifts):
    ne = lax.axis_size("energy")
    reach = max(ne // 4, 1)
    order = green_blocks.shape[1]
    atoms = green_blocks.shape[3]
    nbr = neighbours.shape[0]
    freqs = phonon_shifts.shape[0]
    tiles = atoms // LANES
    share = atoms // ne
    count = order * (order + 1) // 2
    packed = -(-count // 16) * 16
    pad = -(-(tiles * max(nbr - 2, 2)) // 8) * 8
    rows = 16 * (-(-order // 16))
    width = -(-share // LANES) * LANES
    vmem = pl.BlockSpec(memory_space=pltpu.VMEM)
    smem = pl.BlockSpec(memory_space=pltpu.SMEM)
    hbm = pl.BlockSpec(memory_space=pltpu.HBM)
    dma = pltpu.SemaphoreType.DMA
    green = green_blocks[0]
    sigma, summed = pl.pallas_call(
        functools.partial(kernel, reach),
        out_shape=(
            jax.ShapeDtypeStruct((packed, atoms), BF16),
            jax.ShapeDtypeStruct((reach * nbr, width), F32),
        ),
        in_specs=[hbm] * 6,
        out_specs=(vmem, vmem),
        scratch_shapes=[
            pltpu.SMEM((freqs,), jnp.int32),
            pltpu.VMEM((order, order, atoms), BF16),
            pltpu.VMEM((order * order, nbr, atoms), BF16),
            pltpu.VMEM((2 * freqs, nbr, atoms), F32),
            pltpu.VMEM((nbr, atoms), jnp.int32),
            pltpu.VMEM((order * order, packed), BF16),
            pltpu.VMEM((packed, atoms), F32),
            pltpu.VMEM((packed, atoms), BF16),
            pltpu.VMEM((2, packed, atoms), BF16),
            pltpu.VMEM((reach, packed, atoms), BF16),
            pltpu.VMEM((2 * reach, tiles, packed, LANES), BF16),
            pltpu.VMEM((2 * reach, tiles, packed, LANES), BF16),
            pltpu.VMEM((2 * reach, tiles, packed, LANES), F32),
            pltpu.VMEM((ne, reach * nbr, width), F32),
            pltpu.VMEM((ne, reach * nbr, width), F32),
            pltpu.VMEM((2, order, order, pad, LANES), F32),
            pltpu.VMEM((order * order * pad, LANES), F32),
            pltpu.VMEM((2, packed * pad, LANES), F32),
            pltpu.VMEM((2 * reach, nbr, atoms), F32),
            dma((6,)), dma((2,)), dma((2,)), dma((reach,)), dma((reach,)),
            dma((2 * reach, tiles)), dma((2 * reach, tiles)), dma((ne,)), dma((ne,)),
        ],
        compiler_params=pltpu.CompilerParams(
            collective_id=0, has_side_effects=True, vmem_limit_bytes=67043328
        ),
    )(
        phonon_shifts,
        green,
        coupling.reshape(order * order, nbr, atoms),
        phonon_weights.reshape(2 * freqs, nbr, atoms),
        neighbours,
        expansion(order, order, packed),
    )
    corrected, polarization = pl.pallas_call(
        functools.partial(finish, reach),
        out_shape=(
            jax.ShapeDtypeStruct((order, order, atoms), BF16),
            jax.ShapeDtypeStruct((freqs, nbr, share), F32),
        ),
        in_specs=[smem, vmem, vmem, vmem, vmem],
        out_specs=(vmem, vmem),
        scratch_shapes=[pltpu.VMEM((order, rows, atoms), F32)] * 3,
        compiler_params=pltpu.CompilerParams(vmem_limit_bytes=67043328),
    )(phonon_shifts, green, sigma, summed, expansion(order, rows, packed))
    return corrected[None], polarization


def solution(mesh):
    return jax.shard_map(
        body,
        mesh=mesh,
        in_specs=(
            P("energy", None, None, "layer"),
            P(None, None, None, "layer"),
            P(None, None, None, "layer"),
            P(None, "layer"),
            P(),
        ),
        out_specs=(P("energy", None, None, "layer"), P(None, None, ("layer", "energy"))),
        check_vma=False,
    )
```

```python
import functools
import math

import jax
import jax.numpy as jnp
import numpy as np
from jax import lax
from jax.experimental import pallas as pl
from jax.experimental.pallas import tpu as pltpu
from jax.sharding import PartitionSpec as P

MESH = pl.DeviceIdType.MESH
LANES = 128
F32 = jnp.float32
BF16 = jnp.bfloat16


def offsets(order):
    return [p * order - p * (p - 1) // 2 for p in range(order)]


def segments(order, packed):
    plan, start, first = [], 0, 0
    for i in range(0, order, 2):
        done = sum(order - n for n in range(i + 2))
        stop = packed if i + 2 >= order else done // 16 * 16
        if stop - start >= 32 or stop == packed:
            plan.append((start, stop, first, i + 2))
            start, first = stop, i + 2
    return plan


def expansion(order, row_stride, packed_rows):
    off = offsets(order)
    table = np.zeros((order * row_stride, packed_rows), np.float32)
    for p in range(order):
        for q in range(order):
            low, high = min(p, q), max(p, q)
            table[p * row_stride + q, off[low] + high - low] = 1.0
    return jnp.asarray(table, BF16)


def kernel(
    reach, shift_hbm, green_hbm, coup_hbm, weight_hbm, near_hbm, e12_hbm,
    sig_ref, sum_ref,
    shift_ref, green_ref, coup_ref, weight_ref, near_ref, e12_ref, tri32, own, halo, gin, pout, pin, pacc, hots, chunks, cin, c4, g3, pscr, ab,
    load_sem, halo_send, halo_recv, gin_send, gin_recv, part_send, part_recv,
    chunk_send, chunk_recv,
):
    order = green_ref.shape[0]
    atoms = green_ref.shape[2]
    nbr = near_ref.shape[0]
    freqs = shift_ref.shape[0]
    tiles = atoms // LANES
    packed = own.shape[0]
    pad = c4.shape[3]
    ne = lax.axis_size("energy")
    nl = lax.axis_size("layer")
    me = lax.axis_index("energy")
    layer = lax.axis_index("layer")
    share = atoms // ne
    off = offsets(order)
    plan = segments(order, packed)
    groups = (tuple(range(2, nbr)), (0, 1))

    def load(n, src, dst):
        copy = pltpu.make_async_copy(src, dst, load_sem.at[n])
        copy.start()
        return copy

    load_green = load(0, green_hbm, green_ref)
    load_near = load(1, near_hbm, near_ref)
    load_e12 = load(2, e12_hbm, e12_ref)
    load_coup = load(3, coup_hbm, coup_ref)
    load_weight = load(4, weight_hbm, weight_ref)
    load_shift = load(5, shift_hbm, shift_ref)

    barrier = pltpu.get_barrier_semaphore()
    for r in range(1, ne):
        pl.semaphore_signal(
            barrier, inc=1, device_id={"energy": lax.rem(me + r, ne), "layer": layer},
            device_id_type=MESH,
        )

    @pl.when(layer > 0)
    def _():
        pl.semaphore_signal(
            barrier, inc=1, device_id={"energy": me, "layer": layer - 1}, device_id_type=MESH
        )

    @pl.when(layer < nl - 1)
    def _():
        pl.semaphore_signal(
            barrier, inc=1, device_id={"energy": me, "layer": layer + 1}, device_id_type=MESH
        )

    tri32[...] = jnp.zeros_like(tri32)
    load_green.wait()
    for p in range(order):
        tri32[off[p] : off[p] + order - p, :] = green_ref[p].astype(F32)[p:, :]
    own[...] = tri32[...].astype(BF16)

    @pl.when(layer == 0)
    def _():
        halo[0] = jnp.zeros((packed, atoms), BF16)

    @pl.when(layer == nl - 1)
    def _():
        halo[1] = jnp.zeros((packed, atoms), BF16)

    for d in range(1, reach + 1):

        @pl.when(me < d)
        def _():
            gin[d - 1] = jnp.zeros((packed, atoms), BF16)
            pin[2 * d - 2] = jnp.zeros(pin.shape[1:], BF16)

        @pl.when(me + d >= ne)
        def _():
            pin[2 * d - 1] = jnp.zeros(pin.shape[1:], BF16)

    pl.semaphore_wait(
        barrier, ne - 1 + (layer > 0).astype(jnp.int32) + (layer < nl - 1).astype(jnp.int32)
    )

    def remote(src, dst, send, recv, energy, row):
        return pltpu.make_async_remote_copy(
            src_ref=src, dst_ref=dst, send_sem=send, recv_sem=recv,
            device_id={"energy": energy, "layer": row}, device_id_type=MESH,
        )

    def halo_copy(side):
        row = layer + 1 if side == 0 else layer - 1
        return remote(own, halo.at[side], halo_send.at[side], halo_recv.at[side], me, row)

    def green_copy(d):
        return remote(
            own, gin.at[d - 1], gin_send.at[d - 1], gin_recv.at[d - 1], me + d, layer
        )

    def part_copy(slot, n, energy):
        start, stop, _, _ = plan[n]
        rows = pl.ds(start, stop - start)
        return remote(
            pout.at[slot, rows], pin.at[slot, rows], part_send.at[slot, n],
            part_recv.at[slot, n], energy, layer,
        )

    def chunk_copy(r):
        dest = lax.rem(me + r, ne)
        return remote(
            chunks.at[dest], cin.at[r], chunk_send.at[r], chunk_recv.at[r], dest, layer
        )

    has_above, has_below = layer < nl - 1, layer > 0

    @pl.when(has_above)
    def _():
        halo_copy(0).start()

    @pl.when(has_below)
    def _():
        halo_copy(1).start()

    for d in range(1, reach + 1):

        @pl.when(me + d < ne)
        def _():
            green_copy(d).start()

    row = lax.broadcasted_iota(jnp.int32, (atoms, atoms), 0)

    def one_hot(k, start):
        return jnp.where(row == near_ref[k : k + 1, :] - start, 1.0, 0.0).astype(BF16)

    def pick_neighbours(g, j, full, hot):
        size = len(groups[g])
        found = jnp.dot(full, hot, preferred_element_type=F32)
        for t in range(tiles):
            g3[pl.ds(t * size + j, order * order, stride=pad), :] = found[
                :, t * LANES : (t + 1) * LANES
            ]

    def expanded(block):
        return jnp.dot(e12_ref[...], block, preferred_element_type=F32).astype(BF16)

    load_near.wait()
    load_e12.wait()
    own_full = expanded(own[...])
    for j in range(len(groups[0])):
        pick_neighbours(0, j, own_full, one_hot(groups[0][j], atoms))
    hots[0] = one_hot(0, 0)
    hots[1] = one_hot(1, 2 * atoms)

    load_coup.wait()
    for g, slots in enumerate(groups):
        size = len(slots)
        for t in range(tiles):
            block = coup_ref[:, :, t * LANES : (t + 1) * LANES].astype(F32)
            block = block.reshape(order, order, nbr, LANES)
            c4[g, :, :, t * size : (t + 1) * size, :] = block[
                :, :, slots[0] : slots[0] + size, :
            ]

    last = off[-1] + 1
    for g in range(2):
        pscr[g, last * pad :, :] = jnp.zeros(((packed - last) * pad, LANES), F32)

    def products(g, start, stop):
        for i in range(start, stop, 2):
            first = jnp.zeros((2, order, pad, LANES), F32)
            for p in range(order):
                block = g3[p * order * pad : (p + 1) * order * pad, :]
                block = block.reshape(order, pad, LANES)
                first = first + c4[g, i : i + 2, p][:, None] * block[None]
            total = first[:, 0][:, None] * c4[g, i:, 0][None]
            for q in range(1, order):
                total = total + first[:, q][:, None] * c4[g, i:, q][None]
            total = total.astype(BF16).astype(F32)
            for n in range(2):
                pscr[g, off[i + n] * pad : (off[i + n] + order - i - n) * pad, :] = total[
                    n, n:
                ].reshape(-1, LANES)

    products(0, 0, order)

    load_weight.wait()
    load_shift.wait()

    def add_weights(w, sums):
        shift = shift_ref[w]
        low, high = weight_ref[w], weight_ref[freqs + w]
        new = []
        for d in range(1, reach + 1):
            pick = jnp.where(shift == d, 1.0, 0.0).astype(F32)
            new += [sums[2 * d - 2] + pick * low, sums[2 * d - 1] + pick * high]
        return tuple(new)

    sums = lax.fori_loop(
        0, freqs, add_weights, tuple(jnp.zeros((nbr, atoms), F32) for _ in range(2 * reach)),
        unroll=4,
    )
    for s in range(2 * reach):
        ab[s] = sums[s]

    def rows_of(g, t, j, start, stop):
        at = start * pad + t * len(groups[g]) + j
        return pscr[g, pl.ds(at, stop - start, stride=pad), :]

    def partials(g, t, s, start, stop):
        lanes = slice(t * LANES, (t + 1) * LANES)
        total = None
        for j, k in enumerate(groups[g]):
            term = ab[s, k : k + 1, lanes] * rows_of(g, t, j, start, stop)
            total = term if total is None else total + term
        return total

    for t in range(tiles):
        for s in range(2 * reach):
            pacc[s, :, t * LANES : (t + 1) * LANES] = partials(0, t, s, 0, packed)

    for d in range(1, reach + 1):

        @pl.when(me >= d)
        def _():
            green_copy(d).wait_recv()

    index = lax.broadcasted_iota(jnp.int32, (packed, LANES), 0)
    twice = jnp.full((packed, LANES), 2.0, F32)
    for p in range(order):
        twice = jnp.where(index == off[p], 1.0, twice)
    rows = [[None] * tiles for _ in range(reach * nbr)]

    def correlate(g, start, stop):
        for t in range(tiles):
            lanes = slice(t * LANES, (t + 1) * LANES)
            greens = [
                gin[d, start:stop, lanes].astype(F32) * twice[start:stop] for d in range(reach)
            ]
            for j, k in enumerate(groups[g]):
                value = rows_of(g, t, j, start, stop)
                for d in range(reach):
                    term = jnp.sum(greens[d] * value, axis=0, keepdims=True)
                    old = rows[d * nbr + k][t]
                    rows[d * nbr + k][t] = term if old is None else old + term

    correlate(0, 0, packed)

    @pl.when(has_below)
    def _():
        halo_copy(0).wait_recv()

    @pl.when(has_above)
    def _():
        halo_copy(1).wait_recv()

    pick_neighbours(1, 0, expanded(halo[0]), hots[0])
    pick_neighbours(1, 1, expanded(halo[1]), hots[1])
    width = chunks.shape[2]

    for n, (start, stop, first, final) in enumerate(plan):
        products(1, first, final)
        correlate(1, start, stop)
        if stop == packed:
            corr = jnp.concatenate([jnp.concatenate(r, axis=1) for r in rows], axis=0)
            for e in range(ne):
                moved = corr if e == 0 else pltpu.roll(corr, atoms - e * share, 1)
                chunks[e] = moved[:, :width]
            for r in range(1, ne):
                chunk_copy(r).start()
        for t in range(tiles):
            lanes = slice(t * LANES, (t + 1) * LANES)
            for s in range(2 * reach):
                total = pacc[s, start:stop, lanes] + partials(1, t, s, start, stop)
                pout[s, start:stop, lanes] = total.astype(BF16)
        for d in range(1, reach + 1):

            @pl.when(me + d < ne)
            def _():
                part_copy(2 * d - 2, n, me + d).start()

            @pl.when(me >= d)
            def _():
                part_copy(2 * d - 1, n, me - d).start()

    for n, (start, stop, _, _) in enumerate(plan):
        for d in range(1, reach + 1):

            @pl.when(me >= d)
            def _():
                part_copy(2 * d - 2, n, me).wait_recv()

            @pl.when(me + d < ne)
            def _():
                part_copy(2 * d - 1, n, me).wait_recv()

        sigma = pin[0, start:stop].astype(F32)
        for s in range(1, 2 * reach):
            sigma = sigma + pin[s, start:stop].astype(F32)
        sig_ref[start:stop, :] = sigma.astype(BF16)

    for r in range(1, ne):
        chunk_copy(r).wait_recv()
    summed = chunks[me]
    for r in range(1, ne):
        summed = summed + cin[r]
    sum_ref[...] = summed * (1.0 / (order * math.sqrt(ne)))

    @pl.when(has_above)
    def _():
        halo_copy(0).wait_send()

    @pl.when(has_below)
    def _():
        halo_copy(1).wait_send()

    for d in range(1, reach + 1):

        @pl.when(me + d < ne)
        def _():
            green_copy(d).wait_send()
            for n in range(len(plan)):
                part_copy(2 * d - 2, n, me).wait_send()

        @pl.when(me >= d)
        def _():
            for n in range(len(plan)):
                part_copy(2 * d - 1, n, me).wait_send()

    for r in range(1, ne):
        chunk_copy(r).wait_send()


def finish(
    reach, shift_ref, green_ref, sig_ref, sum_ref, e16_ref, out_ref, pol_ref, g16, s16, l16
):
    order = green_ref.shape[0]
    nbr, share = pol_ref.shape[1:]
    freqs = shift_ref.shape[0]
    rows = g16.shape[1]
    s16[...] = jnp.dot(
        e16_ref[...], sig_ref[...], preferred_element_type=F32
    ).reshape(s16.shape)
    g16[...] = jnp.zeros_like(g16)
    for p in range(order):
        g16[p, :order, :] = green_ref[p].astype(F32)

    for i in range(0, order, 2):
        left = [g16[i + n, 0:1, :] * s16[0] for n in range(2)]
        for p in range(1, order):
            block = s16[p]
            left = [left[n] + g16[i + n, p : p + 1, :] * block for n in range(2)]
        for n in range(2):
            l16[i + n] = left[n].astype(BF16).astype(F32)
    for i in range(0, order, 2):
        total = [g16[i + n] for n in range(2)]
        for p in range(order):
            block = g16[p]
            total = [total[n] + l16[i + n, p : p + 1, :] * block for n in range(2)]
        for n in range(2):
            out_ref[i + n] = total[n][:order].astype(BF16)

    summed = sum_ref[:, :share]
    for w in range(freqs):
        shift = shift_ref[w]
        value = jnp.zeros((nbr, share), F32)
        for d in range(1, reach + 1):
            value = jnp.where(shift == d, summed[(d - 1) * nbr : d * nbr], value)
        pol_ref[w] = value


def body(green_blocks, coupling, phonon_weights, neighbours, phonon_shifts):
    ne = lax.axis_size("energy")
    reach = max(ne // 4, 1)
    order = green_blocks.shape[1]
    atoms = green_blocks.shape[3]
    nbr = neighbours.shape[0]
    freqs = phonon_shifts.shape[0]
    tiles = atoms // LANES
    share = atoms // ne
    count = order * (order + 1) // 2
    packed = -(-count // 16) * 16
    pad = -(-(tiles * max(nbr - 2, 2)) // 8) * 8
    rows = 16 * (-(-order // 16))
    width = -(-share // LANES) * LANES
    parts = len(segments(order, packed))
    vmem = pl.BlockSpec(memory_space=pltpu.VMEM)
    smem = pl.BlockSpec(memory_space=pltpu.SMEM)
    hbm = pl.BlockSpec(memory_space=pltpu.HBM)
    dma = pltpu.SemaphoreType.DMA
    green = green_blocks[0]
    sigma, summed = pl.pallas_call(
        functools.partial(kernel, reach),
        out_shape=(
            jax.ShapeDtypeStruct((packed, atoms), BF16),
            jax.ShapeDtypeStruct((reach * nbr, width), F32),
        ),
        in_specs=[hbm] * 6,
        out_specs=(vmem, vmem),
        scratch_shapes=[
            pltpu.SMEM((freqs,), jnp.int32),
            pltpu.VMEM((order, order, atoms), BF16),
            pltpu.VMEM((order * order, nbr, atoms), BF16),
            pltpu.VMEM((2 * freqs, nbr, atoms), F32),
            pltpu.VMEM((nbr, atoms), jnp.int32),
            pltpu.VMEM((order * order, packed), BF16),
            pltpu.VMEM((packed, atoms), F32),
            pltpu.VMEM((packed, atoms), BF16),
            pltpu.VMEM((2, packed, atoms), BF16),
            pltpu.VMEM((reach, packed, atoms), BF16),
            pltpu.VMEM((2 * reach, packed, atoms), BF16),
            pltpu.VMEM((2 * reach, packed, atoms), BF16),
            pltpu.VMEM((2 * reach, packed, atoms), F32),
            pltpu.VMEM((2, atoms, atoms), BF16),
            pltpu.VMEM((ne, reach * nbr, width), F32),
            pltpu.VMEM((ne, reach * nbr, width), F32),
            pltpu.VMEM((2, order, order, pad, LANES), F32),
            pltpu.VMEM((order * order * pad, LANES), F32),
            pltpu.VMEM((2, packed * pad, LANES), F32),
            pltpu.VMEM((2 * reach, nbr, atoms), F32),
            dma((6,)), dma((2,)), dma((2,)), dma((reach,)), dma((reach,)),
            dma((2 * reach, parts)), dma((2 * reach, parts)), dma((ne,)), dma((ne,)),
        ],
        compiler_params=pltpu.CompilerParams(
            collective_id=0, has_side_effects=True, vmem_limit_bytes=67043328
        ),
    )(
        phonon_shifts,
        green,
        coupling.reshape(order * order, nbr, atoms),
        phonon_weights.reshape(2 * freqs, nbr, atoms),
        neighbours,
        expansion(order, order, packed),
    )
    corrected, polarization = pl.pallas_call(
        functools.partial(finish, reach),
        out_shape=(
            jax.ShapeDtypeStruct((order, order, atoms), BF16),
            jax.ShapeDtypeStruct((freqs, nbr, share), F32),
        ),
        in_specs=[smem, vmem, vmem, vmem, vmem],
        out_specs=(vmem, vmem),
        scratch_shapes=[pltpu.VMEM((order, rows, atoms), F32)] * 3,
        compiler_params=pltpu.CompilerParams(vmem_limit_bytes=67043328),
    )(phonon_shifts, green, sigma, summed, expansion(order, rows, packed))
    return corrected[None], polarization


def solution(mesh):
    return jax.shard_map(
        body,
        mesh=mesh,
        in_specs=(
            P("energy", None, None, "layer"),
            P(None, None, None, "layer"),
            P(None, None, None, "layer"),
            P(None, "layer"),
            P(),
        ),
        out_specs=(P("energy", None, None, "layer"), P(None, None, ("layer", "energy"))),
        check_vma=False,
    )
```

```python
import functools
import math

import jax
import jax.numpy as jnp
import numpy as np
from jax import lax
from jax.experimental import pallas as pl
from jax.experimental.pallas import tpu as pltpu
from jax.sharding import PartitionSpec as P

MESH = pl.DeviceIdType.MESH
LANES = 128
F32 = jnp.float32
BF16 = jnp.bfloat16


def offsets(order):
    return [p * order - p * (p - 1) // 2 for p in range(order)]


def segments(order, packed):
    plan, start, first = [], 0, 0
    for i in range(0, order, 2):
        done = sum(order - n for n in range(i + 2))
        stop = packed if i + 2 >= order else done // 16 * 16
        if stop - start >= 32 or stop == packed:
            plan.append((start, stop, first, i + 2))
            start, first = stop, i + 2
    return plan


def expansion(order, row_stride, packed_rows):
    off = offsets(order)
    table = np.zeros((order * row_stride, packed_rows), np.float32)
    for p in range(order):
        for q in range(order):
            low, high = min(p, q), max(p, q)
            table[p * row_stride + q, off[low] + high - low] = 1.0
    return jnp.asarray(table, BF16)


def kernel(
    reach, shift_hbm, green_hbm, coup_hbm, weight_hbm, near_hbm, e12_hbm,
    sig_ref, sum_ref,
    shift_ref, green_ref, coup_ref, weight_ref, near_ref, e12_ref, tri32, own, halo, gin, pout, pin, pacc, hots, chunks, cin, c4, g3, pscr, ab,
    load_sem, hop_sem, halo_send, halo_recv, gin_send, gin_recv, part_send, part_recv,
    chunk_send, chunk_recv,
):
    order = green_ref.shape[0]
    atoms = green_ref.shape[2]
    nbr = near_ref.shape[0]
    freqs = shift_ref.shape[0]
    tiles = atoms // LANES
    packed = own.shape[0]
    pad = c4.shape[3]
    ne = lax.axis_size("energy")
    nl = lax.axis_size("layer")
    me = lax.axis_index("energy")
    layer = lax.axis_index("layer")
    share = atoms // ne
    off = offsets(order)
    plan = segments(order, packed)
    groups = (tuple(range(2, nbr)), (0, 1))

    def load(n, src, dst):
        copy = pltpu.make_async_copy(src, dst, load_sem.at[n])
        copy.start()
        return copy

    load_green = load(0, green_hbm, green_ref)
    load_near = load(1, near_hbm, near_ref)
    load_e12 = load(2, e12_hbm, e12_ref)
    load_coup = load(3, coup_hbm, coup_ref)
    load_weight = load(4, weight_hbm, weight_ref)
    load_shift = load(5, shift_hbm, shift_ref)

    barrier = pltpu.get_barrier_semaphore()

    def greet(sem, energy, row):
        pl.semaphore_signal(
            sem, inc=1, device_id={"energy": energy, "layer": row}, device_id_type=MESH
        )

    def greet_near(sem):
        for d in range(1, reach + 1):

            @pl.when(me + d < ne)
            def _():
                greet(sem, me + d, layer)

            @pl.when(me >= d)
            def _():
                greet(sem, me - d, layer)

    near_count = jnp.minimum(me, reach) + jnp.minimum(ne - 1 - me, reach)
    rounds = -(-(ne - 1) // reach) - 1
    passed = []

    def pass_on():
        n = len(passed)
        if n < rounds:
            pl.semaphore_wait(hop_sem.at[n], near_count)
            if n + 1 < rounds:
                greet_near(hop_sem.at[n + 1])
            passed.append(n)

    greet_near(barrier)

    @pl.when(layer > 0)
    def _():
        pl.semaphore_signal(
            barrier, inc=1, device_id={"energy": me, "layer": layer - 1}, device_id_type=MESH
        )

    @pl.when(layer < nl - 1)
    def _():
        pl.semaphore_signal(
            barrier, inc=1, device_id={"energy": me, "layer": layer + 1}, device_id_type=MESH
        )

    tri32[...] = jnp.zeros_like(tri32)
    load_green.wait()
    for p in range(order):
        tri32[off[p] : off[p] + order - p, :] = green_ref[p].astype(F32)[p:, :]
    own[...] = tri32[...].astype(BF16)

    @pl.when(layer == 0)
    def _():
        halo[0] = jnp.zeros((packed, atoms), BF16)

    @pl.when(layer == nl - 1)
    def _():
        halo[1] = jnp.zeros((packed, atoms), BF16)

    for d in range(1, reach + 1):

        @pl.when(me < d)
        def _():
            gin[d - 1] = jnp.zeros((packed, atoms), BF16)
            pin[2 * d - 2] = jnp.zeros(pin.shape[1:], BF16)

        @pl.when(me + d >= ne)
        def _():
            pin[2 * d - 1] = jnp.zeros(pin.shape[1:], BF16)

    pl.semaphore_wait(
        barrier, near_count + (layer > 0).astype(jnp.int32) + (layer < nl - 1).astype(jnp.int32)
    )

    def remote(src, dst, send, recv, energy, row):
        return pltpu.make_async_remote_copy(
            src_ref=src, dst_ref=dst, send_sem=send, recv_sem=recv,
            device_id={"energy": energy, "layer": row}, device_id_type=MESH,
        )

    def halo_copy(side):
        row = layer + 1 if side == 0 else layer - 1
        return remote(own, halo.at[side], halo_send.at[side], halo_recv.at[side], me, row)

    def green_copy(d):
        return remote(
            own, gin.at[d - 1], gin_send.at[d - 1], gin_recv.at[d - 1], me + d, layer
        )

    def part_copy(slot, n, energy):
        start, stop, _, _ = plan[n]
        rows = pl.ds(start, stop - start)
        return remote(
            pout.at[slot, rows], pin.at[slot, rows], part_send.at[slot, n],
            part_recv.at[slot, n], energy, layer,
        )

    def chunk_copy(r):
        dest = lax.rem(me + r, ne)
        return remote(
            chunks.at[dest], cin.at[r], chunk_send.at[r], chunk_recv.at[r], dest, layer
        )

    has_above, has_below = layer < nl - 1, layer > 0

    @pl.when(has_above)
    def _():
        halo_copy(0).start()

    @pl.when(has_below)
    def _():
        halo_copy(1).start()

    for d in range(1, reach + 1):

        @pl.when(me + d < ne)
        def _():
            green_copy(d).start()

    if rounds:
        greet_near(hop_sem.at[0])

    row = lax.broadcasted_iota(jnp.int32, (atoms, atoms), 0)

    def one_hot(k, start):
        return jnp.where(row == near_ref[k : k + 1, :] - start, 1.0, 0.0).astype(BF16)

    def pick_neighbours(g, j, full, hot):
        size = len(groups[g])
        found = jnp.dot(full, hot, preferred_element_type=F32)
        for t in range(tiles):
            g3[pl.ds(t * size + j, order * order, stride=pad), :] = found[
                :, t * LANES : (t + 1) * LANES
            ]

    def expanded(block):
        return jnp.dot(e12_ref[...], block, preferred_element_type=F32).astype(BF16)

    load_near.wait()
    load_e12.wait()
    own_full = expanded(own[...])
    for j in range(len(groups[0])):
        pick_neighbours(0, j, own_full, one_hot(groups[0][j], atoms))
    hots[0] = one_hot(0, 0)
    hots[1] = one_hot(1, 2 * atoms)

    load_coup.wait()
    for g, slots in enumerate(groups):
        size = len(slots)
        for t in range(tiles):
            block = coup_ref[:, :, t * LANES : (t + 1) * LANES].astype(F32)
            block = block.reshape(order, order, nbr, LANES)
            c4[g, :, :, t * size : (t + 1) * size, :] = block[
                :, :, slots[0] : slots[0] + size, :
            ]

    last = off[-1] + 1
    for g in range(2):
        pscr[g, last * pad :, :] = jnp.zeros(((packed - last) * pad, LANES), F32)

    def products(g, start, stop):
        for i in range(start, stop, 2):
            first = jnp.zeros((2, order, pad, LANES), F32)
            for p in range(order):
                block = g3[p * order * pad : (p + 1) * order * pad, :]
                block = block.reshape(order, pad, LANES)
                first = first + c4[g, i : i + 2, p][:, None] * block[None]
            total = first[:, 0][:, None] * c4[g, i:, 0][None]
            for q in range(1, order):
                total = total + first[:, q][:, None] * c4[g, i:, q][None]
            total = total.astype(BF16).astype(F32)
            for n in range(2):
                pscr[g, off[i + n] * pad : (off[i + n] + order - i - n) * pad, :] = total[
                    n, n:
                ].reshape(-1, LANES)

    products(0, 0, order)

    load_weight.wait()
    load_shift.wait()

    def add_weights(w, sums):
        shift = shift_ref[w]
        low, high = weight_ref[w], weight_ref[freqs + w]
        new = []
        for d in range(1, reach + 1):
            pick = jnp.where(shift == d, 1.0, 0.0).astype(F32)
            new += [sums[2 * d - 2] + pick * low, sums[2 * d - 1] + pick * high]
        return tuple(new)

    sums = lax.fori_loop(
        0, freqs, add_weights, tuple(jnp.zeros((nbr, atoms), F32) for _ in range(2 * reach)),
        unroll=4,
    )
    for s in range(2 * reach):
        ab[s] = sums[s]

    def rows_of(g, t, j, start, stop):
        at = start * pad + t * len(groups[g]) + j
        return pscr[g, pl.ds(at, stop - start, stride=pad), :]

    def partials(g, t, s, start, stop):
        lanes = slice(t * LANES, (t + 1) * LANES)
        total = None
        for j, k in enumerate(groups[g]):
            term = ab[s, k : k + 1, lanes] * rows_of(g, t, j, start, stop)
            total = term if total is None else total + term
        return total

    for t in range(tiles):
        for s in range(2 * reach):
            pacc[s, :, t * LANES : (t + 1) * LANES] = partials(0, t, s, 0, packed)

    for d in range(1, reach + 1):

        @pl.when(me >= d)
        def _():
            green_copy(d).wait_recv()

    index = lax.broadcasted_iota(jnp.int32, (packed, LANES), 0)
    twice = jnp.full((packed, LANES), 2.0, F32)
    for p in range(order):
        twice = jnp.where(index == off[p], 1.0, twice)
    rows = [[None] * tiles for _ in range(reach * nbr)]

    def correlate(g, start, stop):
        for t in range(tiles):
            lanes = slice(t * LANES, (t + 1) * LANES)
            greens = [
                gin[d, start:stop, lanes].astype(F32) * twice[start:stop] for d in range(reach)
            ]
            for j, k in enumerate(groups[g]):
                value = rows_of(g, t, j, start, stop)
                for d in range(reach):
                    term = jnp.sum(greens[d] * value, axis=0, keepdims=True)
                    old = rows[d * nbr + k][t]
                    rows[d * nbr + k][t] = term if old is None else old + term

    correlate(0, 0, packed)

    pass_on()

    @pl.when(has_below)
    def _():
        halo_copy(0).wait_recv()

    @pl.when(has_above)
    def _():
        halo_copy(1).wait_recv()

    pick_neighbours(1, 0, expanded(halo[0]), hots[0])
    pick_neighbours(1, 1, expanded(halo[1]), hots[1])
    width = chunks.shape[2]

    for n, (start, stop, first, final) in enumerate(plan):
        products(1, first, final)
        if n == 0:
            pass_on()
        correlate(1, start, stop)
        if stop == packed:
            while len(passed) < rounds:
                pass_on()
            corr = jnp.concatenate([jnp.concatenate(r, axis=1) for r in rows], axis=0)
            for e in range(ne):
                moved = corr if e == 0 else pltpu.roll(corr, atoms - e * share, 1)
                chunks[e] = moved[:, :width]
            for r in range(1, ne):
                chunk_copy(r).start()
        for t in range(tiles):
            lanes = slice(t * LANES, (t + 1) * LANES)
            for s in range(2 * reach):
                total = pacc[s, start:stop, lanes] + partials(1, t, s, start, stop)
                pout[s, start:stop, lanes] = total.astype(BF16)
        for d in range(1, reach + 1):

            @pl.when(me + d < ne)
            def _():
                part_copy(2 * d - 2, n, me + d).start()

            @pl.when(me >= d)
            def _():
                part_copy(2 * d - 1, n, me - d).start()

    for n, (start, stop, _, _) in enumerate(plan):
        for d in range(1, reach + 1):

            @pl.when(me >= d)
            def _():
                part_copy(2 * d - 2, n, me).wait_recv()

            @pl.when(me + d < ne)
            def _():
                part_copy(2 * d - 1, n, me).wait_recv()

        sigma = pin[0, start:stop].astype(F32)
        for s in range(1, 2 * reach):
            sigma = sigma + pin[s, start:stop].astype(F32)
        sig_ref[start:stop, :] = sigma.astype(BF16)

    for r in range(1, ne):
        chunk_copy(r).wait_recv()
    summed = chunks[me]
    for r in range(1, ne):
        summed = summed + cin[r]
    sum_ref[...] = summed * (1.0 / (order * math.sqrt(ne)))

    @pl.when(has_above)
    def _():
        halo_copy(0).wait_send()

    @pl.when(has_below)
    def _():
        halo_copy(1).wait_send()

    for d in range(1, reach + 1):

        @pl.when(me + d < ne)
        def _():
            green_copy(d).wait_send()
            for n in range(len(plan)):
                part_copy(2 * d - 2, n, me).wait_send()

        @pl.when(me >= d)
        def _():
            for n in range(len(plan)):
                part_copy(2 * d - 1, n, me).wait_send()

    for r in range(1, ne):
        chunk_copy(r).wait_send()


def finish(
    reach, shift_ref, green_ref, sig_ref, sum_ref, e16_ref, out_ref, pol_ref, g16, s16, l16
):
    order = green_ref.shape[0]
    nbr, share = pol_ref.shape[1:]
    freqs = shift_ref.shape[0]
    rows = g16.shape[1]
    s16[...] = jnp.dot(
        e16_ref[...], sig_ref[...], preferred_element_type=F32
    ).reshape(s16.shape)
    g16[...] = jnp.zeros_like(g16)
    for p in range(order):
        g16[p, :order, :] = green_ref[p].astype(F32)

    for i in range(0, order, 2):
        left = [g16[i + n, 0:1, :] * s16[0] for n in range(2)]
        for p in range(1, order):
            block = s16[p]
            left = [left[n] + g16[i + n, p : p + 1, :] * block for n in range(2)]
        for n in range(2):
            l16[i + n] = left[n].astype(BF16).astype(F32)
    for i in range(0, order, 2):
        total = [g16[i + n] for n in range(2)]
        for p in range(order):
            block = g16[p]
            total = [total[n] + l16[i + n, p : p + 1, :] * block for n in range(2)]
        for n in range(2):
            out_ref[i + n] = total[n][:order].astype(BF16)

    summed = sum_ref[:, :share]
    for w in range(freqs):
        shift = shift_ref[w]
        value = jnp.zeros((nbr, share), F32)
        for d in range(1, reach + 1):
            value = jnp.where(shift == d, summed[(d - 1) * nbr : d * nbr], value)
        pol_ref[w] = value


def body(green_blocks, coupling, phonon_weights, neighbours, phonon_shifts):
    ne = lax.axis_size("energy")
    reach = max(ne // 4, 1)
    order = green_blocks.shape[1]
    atoms = green_blocks.shape[3]
    nbr = neighbours.shape[0]
    freqs = phonon_shifts.shape[0]
    tiles = atoms // LANES
    share = atoms // ne
    count = order * (order + 1) // 2
    packed = -(-count // 16) * 16
    pad = -(-(tiles * max(nbr - 2, 2)) // 8) * 8
    rows = 16 * (-(-order // 16))
    width = -(-share // LANES) * LANES
    parts = len(segments(order, packed))
    vmem = pl.BlockSpec(memory_space=pltpu.VMEM)
    smem = pl.BlockSpec(memory_space=pltpu.SMEM)
    hbm = pl.BlockSpec(memory_space=pltpu.HBM)
    dma = pltpu.SemaphoreType.DMA
    green = green_blocks[0]
    sigma, summed = pl.pallas_call(
        functools.partial(kernel, reach),
        out_shape=(
            jax.ShapeDtypeStruct((packed, atoms), BF16),
            jax.ShapeDtypeStruct((reach * nbr, width), F32),
        ),
        in_specs=[hbm] * 6,
        out_specs=(vmem, vmem),
        scratch_shapes=[
            pltpu.SMEM((freqs,), jnp.int32),
            pltpu.VMEM((order, order, atoms), BF16),
            pltpu.VMEM((order * order, nbr, atoms), BF16),
            pltpu.VMEM((2 * freqs, nbr, atoms), F32),
            pltpu.VMEM((nbr, atoms), jnp.int32),
            pltpu.VMEM((order * order, packed), BF16),
            pltpu.VMEM((packed, atoms), F32),
            pltpu.VMEM((packed, atoms), BF16),
            pltpu.VMEM((2, packed, atoms), BF16),
            pltpu.VMEM((reach, packed, atoms), BF16),
            pltpu.VMEM((2 * reach, packed, atoms), BF16),
            pltpu.VMEM((2 * reach, packed, atoms), BF16),
            pltpu.VMEM((2 * reach, packed, atoms), F32),
            pltpu.VMEM((2, atoms, atoms), BF16),
            pltpu.VMEM((ne, reach * nbr, width), F32),
            pltpu.VMEM((ne, reach * nbr, width), F32),
            pltpu.VMEM((2, order, order, pad, LANES), F32),
            pltpu.VMEM((order * order * pad, LANES), F32),
            pltpu.VMEM((2, packed * pad, LANES), F32),
            pltpu.VMEM((2 * reach, nbr, atoms), F32),
            dma((6,)), pltpu.SemaphoreType.REGULAR((max(-(-(ne - 1) // reach) - 1, 1),)),
            dma((2,)), dma((2,)), dma((reach,)), dma((reach,)),
            dma((2 * reach, parts)), dma((2 * reach, parts)), dma((ne,)), dma((ne,)),
        ],
        compiler_params=pltpu.CompilerParams(
            collective_id=0, has_side_effects=True, vmem_limit_bytes=67043328
        ),
    )(
        phonon_shifts,
        green,
        coupling.reshape(order * order, nbr, atoms),
        phonon_weights.reshape(2 * freqs, nbr, atoms),
        neighbours,
        expansion(order, order, packed),
    )
    corrected, polarization = pl.pallas_call(
        functools.partial(finish, reach),
        out_shape=(
            jax.ShapeDtypeStruct((order, order, atoms), BF16),
            jax.ShapeDtypeStruct((freqs, nbr, share), F32),
        ),
        in_specs=[smem, vmem, vmem, vmem, vmem],
        out_specs=(vmem, vmem),
        scratch_shapes=[pltpu.VMEM((order, rows, atoms), F32)] * 3,
        compiler_params=pltpu.CompilerParams(vmem_limit_bytes=67043328),
    )(phonon_shifts, green, sigma, summed, expansion(order, rows, packed))
    return corrected[None], polarization


def solution(mesh):
    return jax.shard_map(
        body,
        mesh=mesh,
        in_specs=(
            P("energy", None, None, "layer"),
            P(None, None, None, "layer"),
            P(None, None, None, "layer"),
            P(None, "layer"),
            P(),
        ),
        out_specs=(P("energy", None, None, "layer"), P(None, None, ("layer", "energy"))),
        check_vma=False,
    )
```

```python
import functools
import math

import jax
import jax.numpy as jnp
import numpy as np
from jax import lax
from jax.experimental import pallas as pl
from jax.experimental.pallas import tpu as pltpu
from jax.sharding import PartitionSpec as P

MESH = pl.DeviceIdType.MESH
LANES = 128
F32 = jnp.float32
BF16 = jnp.bfloat16


def offsets(order):
    return [p * order - p * (p - 1) // 2 for p in range(order)]


def segments(order, packed):
    plan, start, first = [], 0, 0
    for i in range(0, order, 2):
        done = sum(order - n for n in range(i + 2))
        stop = packed if i + 2 >= order else done // 16 * 16
        if stop - start >= 32 or stop == packed:
            plan.append((start, stop, first, i + 2))
            start, first = stop, i + 2
    return plan


def expansion(order, row_stride, packed_rows):
    off = offsets(order)
    table = np.zeros((order * row_stride, packed_rows), np.float32)
    for p in range(order):
        for q in range(order):
            low, high = min(p, q), max(p, q)
            table[p * row_stride + q, off[low] + high - low] = 1.0
    return jnp.asarray(table, BF16)


def kernel(
    reach, shift_hbm, green_hbm, coup_hbm, weight_hbm, near_hbm, e12_hbm,
    e16_hbm, cor_ref, sum_ref,
    shift_ref, green_ref, coup_ref, weight_ref, near_ref, e12_ref, e16_ref, sig_ref,
    g16, s16, l16, tri32, own, halo, gin, pout, pin, pacc, hots, chunks, cin, c4, g3, pscr, ab,
    load_sem, hop_sem, halo_send, halo_recv, gin_send, gin_recv, part_send, part_recv,
    chunk_send, chunk_recv,
):
    order = green_ref.shape[0]
    atoms = green_ref.shape[2]
    nbr = near_ref.shape[0]
    freqs = shift_ref.shape[0]
    tiles = atoms // LANES
    packed = own.shape[0]
    pad = c4.shape[3]
    ne = lax.axis_size("energy")
    nl = lax.axis_size("layer")
    me = lax.axis_index("energy")
    layer = lax.axis_index("layer")
    share = atoms // ne
    off = offsets(order)
    plan = segments(order, packed)
    groups = (tuple(range(2, nbr)), (0, 1))

    def load(n, src, dst):
        copy = pltpu.make_async_copy(src, dst, load_sem.at[n])
        copy.start()
        return copy

    load_green = load(0, green_hbm, green_ref)
    load_near = load(1, near_hbm, near_ref)
    load_e12 = load(2, e12_hbm, e12_ref)
    load_coup = load(3, coup_hbm, coup_ref)
    load_weight = load(4, weight_hbm, weight_ref)
    load_shift = load(5, shift_hbm, shift_ref)
    load_e16 = load(6, e16_hbm, e16_ref)

    barrier = pltpu.get_barrier_semaphore()

    def greet(sem, energy, row):
        pl.semaphore_signal(
            sem, inc=1, device_id={"energy": energy, "layer": row}, device_id_type=MESH
        )

    def greet_near(sem):
        for d in range(1, reach + 1):

            @pl.when(me + d < ne)
            def _():
                greet(sem, me + d, layer)

            @pl.when(me >= d)
            def _():
                greet(sem, me - d, layer)

    near_count = jnp.minimum(me, reach) + jnp.minimum(ne - 1 - me, reach)
    rounds = -(-(ne - 1) // reach) - 1
    passed = []

    def pass_on():
        n = len(passed)
        if n < rounds:
            pl.semaphore_wait(hop_sem.at[n], near_count)
            if n + 1 < rounds:
                greet_near(hop_sem.at[n + 1])
            passed.append(n)

    greet_near(barrier)

    @pl.when(layer > 0)
    def _():
        pl.semaphore_signal(
            barrier, inc=1, device_id={"energy": me, "layer": layer - 1}, device_id_type=MESH
        )

    @pl.when(layer < nl - 1)
    def _():
        pl.semaphore_signal(
            barrier, inc=1, device_id={"energy": me, "layer": layer + 1}, device_id_type=MESH
        )

    tri32[...] = jnp.zeros_like(tri32)
    load_green.wait()
    for p in range(order):
        tri32[off[p] : off[p] + order - p, :] = green_ref[p].astype(F32)[p:, :]
    own[...] = tri32[...].astype(BF16)

    @pl.when(layer == 0)
    def _():
        halo[0] = jnp.zeros((packed, atoms), BF16)

    @pl.when(layer == nl - 1)
    def _():
        halo[1] = jnp.zeros((packed, atoms), BF16)

    for d in range(1, reach + 1):

        @pl.when(me < d)
        def _():
            gin[d - 1] = jnp.zeros((packed, atoms), BF16)
            pin[2 * d - 2] = jnp.zeros(pin.shape[1:], BF16)

        @pl.when(me + d >= ne)
        def _():
            pin[2 * d - 1] = jnp.zeros(pin.shape[1:], BF16)

    pl.semaphore_wait(
        barrier, near_count + (layer > 0).astype(jnp.int32) + (layer < nl - 1).astype(jnp.int32)
    )

    def remote(src, dst, send, recv, energy, row):
        return pltpu.make_async_remote_copy(
            src_ref=src, dst_ref=dst, send_sem=send, recv_sem=recv,
            device_id={"energy": energy, "layer": row}, device_id_type=MESH,
        )

    def halo_copy(side):
        row = layer + 1 if side == 0 else layer - 1
        return remote(own, halo.at[side], halo_send.at[side], halo_recv.at[side], me, row)

    def green_copy(d):
        return remote(
            own, gin.at[d - 1], gin_send.at[d - 1], gin_recv.at[d - 1], me + d, layer
        )

    def part_copy(slot, n, energy):
        start, stop, _, _ = plan[n]
        rows = pl.ds(start, stop - start)
        return remote(
            pout.at[slot, rows], pin.at[slot, rows], part_send.at[slot, n],
            part_recv.at[slot, n], energy, layer,
        )

    def chunk_copy(r):
        dest = lax.rem(me + r, ne)
        return remote(
            chunks.at[dest], cin.at[r], chunk_send.at[r], chunk_recv.at[r], dest, layer
        )

    has_above, has_below = layer < nl - 1, layer > 0

    @pl.when(has_above)
    def _():
        halo_copy(0).start()

    @pl.when(has_below)
    def _():
        halo_copy(1).start()

    for d in range(1, reach + 1):

        @pl.when(me + d < ne)
        def _():
            green_copy(d).start()

    if rounds:
        greet_near(hop_sem.at[0])

    row = lax.broadcasted_iota(jnp.int32, (atoms, atoms), 0)

    def one_hot(k, start):
        return jnp.where(row == near_ref[k : k + 1, :] - start, 1.0, 0.0).astype(BF16)

    def pick_neighbours(g, j, full, hot):
        size = len(groups[g])
        found = jnp.dot(full, hot, preferred_element_type=F32)
        for t in range(tiles):
            g3[pl.ds(t * size + j, order * order, stride=pad), :] = found[
                :, t * LANES : (t + 1) * LANES
            ]

    def expanded(block):
        return jnp.dot(e12_ref[...], block, preferred_element_type=F32).astype(BF16)

    load_near.wait()
    load_e12.wait()
    own_full = expanded(own[...])
    for j in range(len(groups[0])):
        pick_neighbours(0, j, own_full, one_hot(groups[0][j], atoms))
    hots[0] = one_hot(0, 0)
    hots[1] = one_hot(1, 2 * atoms)

    load_coup.wait()
    for g, slots in enumerate(groups):
        size = len(slots)
        for t in range(tiles):
            block = coup_ref[:, :, t * LANES : (t + 1) * LANES].astype(F32)
            block = block.reshape(order, order, nbr, LANES)
            c4[g, :, :, t * size : (t + 1) * size, :] = block[
                :, :, slots[0] : slots[0] + size, :
            ]

    last = off[-1] + 1
    for g in range(2):
        pscr[g, last * pad :, :] = jnp.zeros(((packed - last) * pad, LANES), F32)

    def products(g, start, stop):
        for i in range(start, stop, 2):
            first = jnp.zeros((2, order, pad, LANES), F32)
            for p in range(order):
                block = g3[p * order * pad : (p + 1) * order * pad, :]
                block = block.reshape(order, pad, LANES)
                first = first + c4[g, i : i + 2, p][:, None] * block[None]
            total = first[:, 0][:, None] * c4[g, i:, 0][None]
            for q in range(1, order):
                total = total + first[:, q][:, None] * c4[g, i:, q][None]
            total = total.astype(BF16).astype(F32)
            for n in range(2):
                pscr[g, off[i + n] * pad : (off[i + n] + order - i - n) * pad, :] = total[
                    n, n:
                ].reshape(-1, LANES)

    products(0, 0, order)

    load_weight.wait()
    load_shift.wait()

    def add_weights(w, sums):
        shift = shift_ref[w]
        low, high = weight_ref[w], weight_ref[freqs + w]
        new = []
        for d in range(1, reach + 1):
            pick = jnp.where(shift == d, 1.0, 0.0).astype(F32)
            new += [sums[2 * d - 2] + pick * low, sums[2 * d - 1] + pick * high]
        return tuple(new)

    sums = lax.fori_loop(
        0, freqs, add_weights, tuple(jnp.zeros((nbr, atoms), F32) for _ in range(2 * reach)),
        unroll=4,
    )
    for s in range(2 * reach):
        ab[s] = sums[s]

    def rows_of(g, t, j, start, stop):
        at = start * pad + t * len(groups[g]) + j
        return pscr[g, pl.ds(at, stop - start, stride=pad), :]

    def partials(g, t, s, start, stop):
        lanes = slice(t * LANES, (t + 1) * LANES)
        total = None
        for j, k in enumerate(groups[g]):
            term = ab[s, k : k + 1, lanes] * rows_of(g, t, j, start, stop)
            total = term if total is None else total + term
        return total

    for t in range(tiles):
        for s in range(2 * reach):
            pacc[s, :, t * LANES : (t + 1) * LANES] = partials(0, t, s, 0, packed)

    for d in range(1, reach + 1):

        @pl.when(me >= d)
        def _():
            green_copy(d).wait_recv()

    index = lax.broadcasted_iota(jnp.int32, (packed, LANES), 0)
    twice = jnp.full((packed, LANES), 2.0, F32)
    for p in range(order):
        twice = jnp.where(index == off[p], 1.0, twice)
    rows = [[None] * tiles for _ in range(reach * nbr)]

    def correlate(g, start, stop):
        for t in range(tiles):
            lanes = slice(t * LANES, (t + 1) * LANES)
            greens = [
                gin[d, start:stop, lanes].astype(F32) * twice[start:stop] for d in range(reach)
            ]
            for j, k in enumerate(groups[g]):
                value = rows_of(g, t, j, start, stop)
                for d in range(reach):
                    term = jnp.sum(greens[d] * value, axis=0, keepdims=True)
                    old = rows[d * nbr + k][t]
                    rows[d * nbr + k][t] = term if old is None else old + term

    correlate(0, 0, packed)

    pass_on()
    load_e16.wait()
    g16[...] = jnp.zeros_like(g16)
    for p in range(order):
        g16[p, :order, :] = green_ref[p].astype(F32)

    @pl.when(has_below)
    def _():
        halo_copy(0).wait_recv()

    @pl.when(has_above)
    def _():
        halo_copy(1).wait_recv()

    pick_neighbours(1, 0, expanded(halo[0]), hots[0])
    pick_neighbours(1, 1, expanded(halo[1]), hots[1])
    width = chunks.shape[2]

    for n, (start, stop, first, final) in enumerate(plan):
        products(1, first, final)
        if n == 0:
            pass_on()
        correlate(1, start, stop)
        if stop == packed:
            while len(passed) < rounds:
                pass_on()
            corr = jnp.concatenate([jnp.concatenate(r, axis=1) for r in rows], axis=0)
            for e in range(ne):
                moved = corr if e == 0 else pltpu.roll(corr, atoms - e * share, 1)
                chunks[e] = moved[:, :width]
            for r in range(1, ne):
                chunk_copy(r).start()
        for t in range(tiles):
            lanes = slice(t * LANES, (t + 1) * LANES)
            for s in range(2 * reach):
                total = pacc[s, start:stop, lanes] + partials(1, t, s, start, stop)
                pout[s, start:stop, lanes] = total.astype(BF16)
        for d in range(1, reach + 1):

            @pl.when(me + d < ne)
            def _():
                part_copy(2 * d - 2, n, me + d).start()

            @pl.when(me >= d)
            def _():
                part_copy(2 * d - 1, n, me - d).start()

    for n, (start, stop, _, _) in enumerate(plan):
        for d in range(1, reach + 1):

            @pl.when(me >= d)
            def _():
                part_copy(2 * d - 2, n, me).wait_recv()

            @pl.when(me + d < ne)
            def _():
                part_copy(2 * d - 1, n, me).wait_recv()

        sigma = pin[0, start:stop].astype(F32)
        for s in range(1, 2 * reach):
            sigma = sigma + pin[s, start:stop].astype(F32)
        sig_ref[start:stop, :] = sigma.astype(BF16)

    s16[...] = jnp.dot(
        e16_ref[...], sig_ref[...], preferred_element_type=F32
    ).reshape(s16.shape)

    for i in range(0, order, 2):
        left = [g16[i + n, 0:1, :] * s16[0] for n in range(2)]
        for p in range(1, order):
            block = s16[p]
            left = [left[n] + g16[i + n, p : p + 1, :] * block for n in range(2)]
        for n in range(2):
            l16[i + n] = left[n].astype(BF16).astype(F32)
    for i in range(0, order, 2):
        total = [g16[i + n] for n in range(2)]
        for p in range(order):
            block = g16[p]
            total = [total[n] + l16[i + n, p : p + 1, :] * block for n in range(2)]
        for n in range(2):
            cor_ref[i + n] = total[n][:order].astype(BF16)

    for r in range(1, ne):
        chunk_copy(r).wait_recv()
    summed = chunks[me]
    for r in range(1, ne):
        summed = summed + cin[r]
    sum_ref[...] = summed * (1.0 / (order * math.sqrt(ne)))

    @pl.when(has_above)
    def _():
        halo_copy(0).wait_send()

    @pl.when(has_below)
    def _():
        halo_copy(1).wait_send()

    for d in range(1, reach + 1):

        @pl.when(me + d < ne)
        def _():
            green_copy(d).wait_send()
            for n in range(len(plan)):
                part_copy(2 * d - 2, n, me).wait_send()

        @pl.when(me >= d)
        def _():
            for n in range(len(plan)):
                part_copy(2 * d - 1, n, me).wait_send()

    for r in range(1, ne):
        chunk_copy(r).wait_send()


def finish(reach, shift_ref, cor_ref, sum_ref, out_ref, pol_ref):
    nbr, share = pol_ref.shape[1:]
    freqs = shift_ref.shape[0]
    out_ref[...] = cor_ref[...]
    summed = sum_ref[:, :share]
    for w in range(freqs):
        shift = shift_ref[w]
        value = jnp.zeros((nbr, share), F32)
        for d in range(1, reach + 1):
            value = jnp.where(shift == d, summed[(d - 1) * nbr : d * nbr], value)
        pol_ref[w] = value


def body(green_blocks, coupling, phonon_weights, neighbours, phonon_shifts):
    ne = lax.axis_size("energy")
    reach = max(ne // 4, 1)
    order = green_blocks.shape[1]
    atoms = green_blocks.shape[3]
    nbr = neighbours.shape[0]
    freqs = phonon_shifts.shape[0]
    tiles = atoms // LANES
    share = atoms // ne
    count = order * (order + 1) // 2
    packed = -(-count // 16) * 16
    pad = -(-(tiles * max(nbr - 2, 2)) // 8) * 8
    rows = 16 * (-(-order // 16))
    width = -(-share // LANES) * LANES
    parts = len(segments(order, packed))
    vmem = pl.BlockSpec(memory_space=pltpu.VMEM)
    smem = pl.BlockSpec(memory_space=pltpu.SMEM)
    hbm = pl.BlockSpec(memory_space=pltpu.HBM)
    dma = pltpu.SemaphoreType.DMA
    green = green_blocks[0]
    result, summed = pl.pallas_call(
        functools.partial(kernel, reach),
        out_shape=(
            jax.ShapeDtypeStruct((order, order, atoms), BF16),
            jax.ShapeDtypeStruct((reach * nbr, width), F32),
        ),
        in_specs=[hbm] * 7,
        out_specs=(vmem, vmem),
        scratch_shapes=[
            pltpu.SMEM((freqs,), jnp.int32),
            pltpu.VMEM((order, order, atoms), BF16),
            pltpu.VMEM((order * order, nbr, atoms), BF16),
            pltpu.VMEM((2 * freqs, nbr, atoms), F32),
            pltpu.VMEM((nbr, atoms), jnp.int32),
            pltpu.VMEM((order * order, packed), BF16),
            pltpu.VMEM((order * rows, packed), BF16),
            pltpu.VMEM((packed, atoms), BF16),
            pltpu.VMEM((order, rows, atoms), F32),
            pltpu.VMEM((order, rows, atoms), F32),
            pltpu.VMEM((order, rows, atoms), F32),
            pltpu.VMEM((packed, atoms), F32),
            pltpu.VMEM((packed, atoms), BF16),
            pltpu.VMEM((2, packed, atoms), BF16),
            pltpu.VMEM((reach, packed, atoms), BF16),
            pltpu.VMEM((2 * reach, packed, atoms), BF16),
            pltpu.VMEM((2 * reach, packed, atoms), BF16),
            pltpu.VMEM((2 * reach, packed, atoms), F32),
            pltpu.VMEM((2, atoms, atoms), BF16),
            pltpu.VMEM((ne, reach * nbr, width), F32),
            pltpu.VMEM((ne, reach * nbr, width), F32),
            pltpu.VMEM((2, order, order, pad, LANES), F32),
            pltpu.VMEM((order * order * pad, LANES), F32),
            pltpu.VMEM((2, packed * pad, LANES), F32),
            pltpu.VMEM((2 * reach, nbr, atoms), F32),
            dma((7,)), pltpu.SemaphoreType.REGULAR((max(-(-(ne - 1) // reach) - 1, 1),)),
            dma((2,)), dma((2,)), dma((reach,)), dma((reach,)),
            dma((2 * reach, parts)), dma((2 * reach, parts)), dma((ne,)), dma((ne,)),
        ],
        compiler_params=pltpu.CompilerParams(
            collective_id=0, has_side_effects=True, vmem_limit_bytes=67043328
        ),
    )(
        phonon_shifts,
        green,
        coupling.reshape(order * order, nbr, atoms),
        phonon_weights.reshape(2 * freqs, nbr, atoms),
        neighbours,
        expansion(order, order, packed),
        expansion(order, rows, packed),
    )
    corrected, polarization = pl.pallas_call(
        functools.partial(finish, reach),
        out_shape=(
            jax.ShapeDtypeStruct((order, order, atoms), BF16),
            jax.ShapeDtypeStruct((freqs, nbr, share), F32),
        ),
        in_specs=[smem, vmem, vmem],
        out_specs=(vmem, vmem),
        compiler_params=pltpu.CompilerParams(vmem_limit_bytes=67043328),
    )(phonon_shifts, result, summed)
    return corrected[None], polarization


def solution(mesh):
    return jax.shard_map(
        body,
        mesh=mesh,
        in_specs=(
            P("energy", None, None, "layer"),
            P(None, None, None, "layer"),
            P(None, None, None, "layer"),
            P(None, "layer"),
            P(),
        ),
        out_specs=(P("energy", None, None, "layer"), P(None, None, ("layer", "energy"))),
        check_vma=False,
    )
```
